256 devices in a mesh: gx: 8 (over x, y_lo), gy: 32 (over y_hi, z, core).
Axes of the slice: x: 4, y: 4 (y_hi: 2, y_lo: 2; y = y_hi * 2 + y_lo), z: 8, core: 2. Of those that a mesh axis runs over, the one named last changes fastest.
Arguments:
- fields: bfloat16 [64, 512, 1024], P('gx', 'gy'), may hold values from -6 to 6
- grad_out: bfloat16 [64, 512, 1024], P('gx', 'gy'), may hold values from -6 to 6
- norm_gain: float32 [1024], replicated, may hold values from 0.25 to 1.75
- w_qkv: bfloat16 [1024, 3072], replicated, may hold values from -3 to 3
- brick_mask: int32 [8, 64, 8], P('gx', 'gy'), may hold values 0 or 1
Outputs:
- output: bfloat16 [64, 512, 1024], P('gx', 'gy')
- grad_in: bfloat16 [64, 512, 1024], P('gx', 'gy')
- w_grad_qkv: float32 [1024, 3072], P(('gx', 'gy'))
- gain_grad: float32 [1024], P(('gx', 'gy'))
The draws below stay inside these ranges and needn't reach their ends.
All inputs are finite; a program needn't handle non-finite values. No bound on the sum of `brick_mask` on one device may be relied on, other than what follows from the above.
Results may differ from the reference program's by a relative error of at most 0.017.
The reference program's roundings to bfloat16 on the way count: a program that leaves them out, or rounds other values in their place, can miss the bound.
Values may be sent and summed in bfloat16 or wider, within the bound.
A program may use at most 128 MiB of HBM per device.

```python
import jax
import jax.numpy as jnp
from jax import lax

D = 1024
HEADS = 16
BRICK = 8
NBX = 8
NBY = 64
NX = 64
NY = 512


def draw_w_qkv(key, part):
    spread = (D // 4) ** (-0.5)
    drawn = jax.random.normal(key, (D, 3 * D), jnp.float32) * spread
    return jnp.clip(drawn, -3.0, 3.0).astype(jnp.bfloat16)


def with_ends(result, own_key, least, top_value):
    index_at = [jax.random.randint(jax.random.fold_in(own_key, axis), (), 0, length) for axis, length in enumerate(result.shape)]
    longest = result.shape.index(max(result.shape))
    neighbour = index_at[:longest] + [(index_at[longest] + 1) % result.shape[longest]] + index_at[longest + 1:]
    return result.at[tuple(index_at)].set(least).at[tuple(neighbour)].set(top_value)


def block_scale(key, extent, shards, smallest, top_value):
    def one(position, shards_of):
        heights = jax.random.uniform(jax.random.fold_in(jax.random.fold_in(key, 6), position), (shards_of,), jnp.float32, smallest / len(shards), top_value / len(shards))
        return jnp.repeat(jnp.exp(heights), extent[position] // shards_of).reshape((-1,) + (1,) * (len(extent) - position - 1))

    gain = one(*shards[0])
    for cut in shards[1:]:
        gain = gain * one(*cut)
    return gain


def normal_values(own_key, shape, deviation, bound, cuts=(), held_as=jnp.bfloat16):
    entries = jax.random.normal(own_key, shape, jnp.float32) * deviation
    if len(cuts) > 0:
        entries = block_scale(own_key, shape, cuts, -0.22, 0.18) * entries
    return jnp.clip(entries, min=-bound, max=bound).astype(held_as)


def setup_inputs(seed: int = 0) -> dict:
    key_list = jax.random.split(jax.random.key(seed), 6)
    return {
        "fields": normal_values(key_list[0], (NX, NY, D), 1.0, 6.0, ((0, 8), (1, 32))),
        "grad_out": normal_values(key_list[1], (NX, NY, D), 1.0, 6.0, ((0, 8), (1, 32))),
        "norm_gain": jnp.clip(1.0 + 0.15 * jax.random.normal(key_list[2], (D,), jnp.float32), 0.25, 1.75),
        "w_qkv": draw_w_qkv(jax.random.fold_in(key_list[5], 71), 0),
        "brick_mask": with_ends((jax.random.randint(key_list[4], (NBX, NBY, 8), 0, 4) < 3).astype(jnp.int32), jax.random.fold_in(key_list[4], 1), 0, 1),
    }


EPSILON = 1e-05
NEG_BIG = -1e+30

def to_bricks(table):
    tile_rows, tile_cols, channels = table.shape
    shaped = table.reshape(tile_rows // BRICK, BRICK, tile_cols // BRICK, BRICK, channels)
    return shaped.transpose(0, 2, 1, 3, 4).reshape(tile_rows // BRICK, tile_cols // BRICK, BRICK * BRICK, channels)

def from_bricks(blocks):
    b_rows, b_cols, inside, channels = blocks.shape
    shaped = blocks.reshape(b_rows, b_cols, BRICK, BRICK, channels)
    return shaped.transpose(0, 2, 1, 3, 4).reshape(b_rows * BRICK, b_cols * BRICK, channels)

def windows(extended, tile_rows, tile_cols):
    pieces = []
    for row_step in range(3):
        for col_step in range(3):
            pieces.append(to_bricks(extended[BRICK * row_step:BRICK * row_step + tile_rows, BRICK * col_step:BRICK * col_step + tile_cols]))
    stacked = jnp.stack(pieces, axis=2)
    return stacked.reshape(stacked.shape[0], stacked.shape[1], 9 * BRICK * BRICK, stacked.shape[-1])

def allowed_keys(mask_tile):
    ones_col = jnp.ones(mask_tile.shape[:2] + (1,), jnp.int32)
    all_nine = jnp.concatenate([mask_tile[:, :, :4], ones_col, mask_tile[:, :, 4:]], axis=2)
    spread = jnp.broadcast_to(all_nine[:, :, :, None], all_nine.shape + (BRICK * BRICK,))
    return spread.reshape(all_nine.shape[0], all_nine.shape[1], 9 * BRICK * BRICK) > 0

def spread_back(grad_win, tile_rows, tile_cols):
    b_rows, b_cols, keys_all, channels = grad_win.shape
    shaped = grad_win.reshape(b_rows, b_cols, 9, BRICK * BRICK, channels)
    ext_grad = jnp.zeros((tile_rows + 2 * BRICK, tile_cols + 2 * BRICK, channels), jnp.float32)
    for row_step in range(3):
        for col_step in range(3):
            piece = from_bricks(shaped[:, :, 3 * row_step + col_step])
            ext_grad = ext_grad.at[BRICK * row_step:BRICK * row_step + tile_rows, BRICK * col_step:BRICK * col_step + tile_cols].add(piece)
    return ext_grad

def attend_both(q_tile, ext_tile, grad_tile, mask_tile):
    tile_rows, tile_cols, feat_width = q_tile.shape
    head_dim = feat_width // HEADS
    scale_qk = head_dim ** (-0.5)
    q_bricks = to_bricks(q_tile)
    b_rows, b_cols = (q_bricks.shape[0], q_bricks.shape[1])
    inside = BRICK * BRICK
    head_q = q_bricks.reshape(b_rows, b_cols, inside, HEADS, head_dim).astype(jnp.float32)
    key_win = windows(ext_tile, tile_rows, tile_cols)
    head_k = key_win[..., :feat_width].reshape(b_rows, b_cols, 9 * inside, HEADS, head_dim).astype(jnp.float32)
    head_v = key_win[..., feat_width:].reshape(b_rows, b_cols, 9 * inside, HEADS, head_dim).astype(jnp.float32)
    scores = jnp.einsum('abqhd,abkhd->abhqk', head_q, head_k) * scale_qk
    allowed = allowed_keys(mask_tile)
    scores = jnp.where(allowed[:, :, None, None, :], scores, NEG_BIG)
    row_max = lax.optimization_barrier(jnp.max(scores, axis=-1, keepdims=True))
    exp_s = jnp.exp(scores - row_max)
    prob_f = exp_s / lax.optimization_barrier(jnp.sum(exp_s, axis=-1, keepdims=True))
    weights = prob_f.astype(jnp.bfloat16)
    mixed_f = jnp.einsum('abhqk,abkhd->abqhd', weights.astype(jnp.float32), head_v)
    mixed_b = mixed_f.astype(jnp.bfloat16).reshape(b_rows, b_cols, inside, feat_width)
    grad_head = to_bricks(grad_tile).reshape(b_rows, b_cols, inside, HEADS, head_dim).astype(jnp.float32)
    grad_prob = jnp.einsum('abqhd,abkhd->abhqk', grad_head, head_v)
    inner_sum = lax.optimization_barrier(jnp.sum(prob_f * grad_prob, axis=-1, keepdims=True))
    grad_score = (prob_f * (grad_prob - inner_sum) * scale_qk).astype(jnp.bfloat16).astype(jnp.float32)
    grad_q = jnp.einsum('abhqk,abkhd->abqhd', grad_score, head_k).astype(jnp.bfloat16)
    grad_k = jnp.einsum('abhqk,abqhd->abkhd', grad_score, head_q)
    grad_v = jnp.einsum('abhqk,abqhd->abkhd', weights.astype(jnp.float32), grad_head)
    grad_win = jnp.concatenate([grad_k.reshape(b_rows, b_cols, 9 * inside, feat_width), grad_v.reshape(b_rows, b_cols, 9 * inside, feat_width)], axis=-1)
    grad_q = grad_q.reshape(b_rows, b_cols, inside, feat_width)
    return (from_bricks(mixed_b), from_bricks(grad_q), grad_win)

def reference(fields, grad_out, norm_gain, w_qkv, brick_mask):
    grid_rows, grid_cols, feat_width = fields.shape
    tok_count = grid_rows * grid_cols
    flat_in = fields.reshape(tok_count, feat_width).astype(jnp.float32)
    inv_rms = lax.rsqrt(lax.optimization_barrier(jnp.mean(flat_in * flat_in, axis=1, keepdims=True)) + EPSILON)
    normed = (flat_in * inv_rms * norm_gain).astype(jnp.bfloat16)
    proj_all = jnp.dot(normed, w_qkv, preferred_element_type=jnp.float32).astype(jnp.bfloat16)
    queries = proj_all[:, :feat_width].reshape(grid_rows, grid_cols, feat_width)
    keyval = proj_all[:, feat_width:].reshape(grid_rows, grid_cols, 2 * feat_width)
    padded = jnp.pad(keyval, ((BRICK, BRICK), (BRICK, BRICK), (0, 0)), mode='wrap')
    grad_flat = grad_out.reshape(tok_count, feat_width)
    strips = grid_rows // BRICK

    def one_strip(grad_pad, strip_idx):
        row_start = (strip_idx * BRICK).astype(jnp.int32)
        q_strip = lax.dynamic_slice_in_dim(queries, row_start, BRICK, 0)
        ext_strip = lax.dynamic_slice_in_dim(padded, row_start, 3 * BRICK, 0)
        g_strip = lax.dynamic_slice_in_dim(grad_out, row_start, BRICK, 0)
        m_strip = lax.dynamic_slice_in_dim(brick_mask, strip_idx.astype(jnp.int32), 1, 0)
        mixed_b, grad_q, grad_win = attend_both(q_strip, ext_strip, g_strip, m_strip)
        ext_grad = spread_back(grad_win, BRICK, grid_cols)
        current = lax.dynamic_slice_in_dim(grad_pad, row_start, 3 * BRICK, 0)
        grad_pad = lax.dynamic_update_slice_in_dim(grad_pad, current + ext_grad, row_start, 0)
        return (grad_pad, (mixed_b, grad_q))
    grad_zero = jnp.zeros(padded.shape, jnp.float32)
    grad_pad, (mixed_all, grad_q_all) = lax.scan(one_strip, grad_zero, jnp.arange(strips, dtype=jnp.int32))
    inner = grad_pad[:, BRICK:-BRICK]
    inner = inner.at[:, :BRICK].add(grad_pad[:, -BRICK:]).at[:, -BRICK:].add(grad_pad[:, :BRICK])
    core = inner[BRICK:-BRICK]
    core = core.at[:BRICK].add(inner[-BRICK:]).at[-BRICK:].add(inner[:BRICK])
    grad_kv = core.astype(jnp.bfloat16).reshape(tok_count, 2 * feat_width)
    grad_qkv = jnp.concatenate([grad_q_all.reshape(tok_count, feat_width), grad_kv], axis=1)
    attn_flat = mixed_all.reshape(tok_count, feat_width)
    output = (flat_in + attn_flat.astype(jnp.float32)).astype(jnp.bfloat16).reshape(fields.shape)
    grad_normed = lax.dot_general(grad_qkv, w_qkv, (((1,), (1,)), ((), ())), preferred_element_type=jnp.float32)
    inv_tokens = tok_count ** (-0.5)
    w_grad_qkv = lax.dot_general(normed, grad_qkv, (((0,), (0,)), ((), ())), preferred_element_type=jnp.float32) * inv_tokens
    gain_grad = lax.optimization_barrier(jnp.sum(grad_normed * flat_in * inv_rms, axis=0)) * inv_tokens
    scaled = grad_normed * norm_gain
    grad_in = grad_flat.astype(jnp.float32) + inv_rms * (scaled - flat_in * inv_rms * inv_rms * lax.optimization_barrier(jnp.mean(scaled * flat_in, axis=1, keepdims=True)))
    grad_in = grad_in.astype(jnp.bfloat16).reshape(fields.shape)
    return (output, grad_in, w_grad_qkv, gain_grad)
```

```python
import jax
import jax.numpy as jnp
from jax import lax
from jax.experimental import pallas as pl
from jax.experimental.pallas import tpu as pltpu
from jax.sharding import PartitionSpec as P

HEADS = 16
BRICK = 8
D = 1024
HD = 64
GROUP = 4
GW = GROUP * HD
INSIDE = BRICK * BRICK
OWN = 2 * INSIDE
EXT = 12 * INSIDE
EPSILON = 1e-05
NEG_BIG = -1e30
SCALE = HD ** (-0.5)
ALL_TOKENS = 32768
MESH = pl.DeviceIdType.MESH
F32 = jnp.float32
BF16 = jnp.bfloat16
ANY = pl.BlockSpec(memory_space=pl.ANY)
VM = pl.BlockSpec(memory_space=pltpu.VMEM)
VMEM_LIMIT = 56 * 1024 * 1024

COLUMN_OF = (1, 2, 3, 0)


def brick_of(tile, b):
    part = tile[:, BRICK * b : BRICK * (b + 1), :]
    return part.reshape(INSIDE, part.shape[-1])


def tile_of(bricks):
    width = bricks.shape[-1]
    first = bricks[:INSIDE].reshape(BRICK, BRICK, width)
    second = bricks[INSIDE:].reshape(BRICK, BRICK, width)
    return jnp.concatenate([first, second], axis=1)


def norm_kernel(fields_ref, grad_ref, gain_ref, nb_ref, nt_ref, gb_ref):
    x = fields_ref[...].astype(F32)
    x = jnp.concatenate([brick_of(x, 0), brick_of(x, 1)], axis=0)
    inv = lax.rsqrt(jnp.mean(x * x, axis=1, keepdims=True) + EPSILON)
    n = (x * inv * gain_ref[...]).astype(BF16)
    nb_ref[...] = n.reshape(2, INSIDE, D)
    nt_ref[...] = jnp.transpose(n.astype(F32)).astype(BF16)
    g = grad_ref[...].astype(F32)
    g = jnp.concatenate([brick_of(g, 0), brick_of(g, 1)], axis=0)
    gb_ref[...] = g.astype(BF16).reshape(2, INSIDE, D)


def norm_call(fields, grad_out, gain):
    return pl.pallas_call(
        norm_kernel,
        out_shape=(
            jax.ShapeDtypeStruct((2, INSIDE, D), BF16),
            jax.ShapeDtypeStruct((D, OWN), BF16),
            jax.ShapeDtypeStruct((2, INSIDE, D), BF16),
        ),
        in_specs=[VM] * 3,
        out_specs=(VM,) * 3,
        name="norm",
    )(fields, grad_out, gain)


def shifted(gx, gy, dx, dy):
    nx, ny = lax.axis_size("gx"), lax.axis_size("gy")
    return {"gx": lax.rem(gx + dx + nx, nx), "gy": lax.rem(gy + dy + ny, ny)}


def meet(peers):
    barrier = pltpu.get_barrier_semaphore()
    for peer in peers:
        pl.semaphore_signal(barrier, inc=1, device_id=peer, device_id_type=MESH)
    pl.semaphore_wait(barrier, len(peers))


def halo_kernel(nb, gb, nt, nrow, ncol, grow, gcol, ntp, send, recv):
    gx, gy = lax.axis_index("gx"), lax.axis_index("gy")
    up, down = shifted(gx, gy, -1, 0), shifted(gx, gy, 1, 0)
    left, right = shifted(gx, gy, 0, -1), shifted(gx, gy, 0, 1)
    partner = {"gx": gx, "gy": gy + 1 - 2 * lax.rem(gy, 2)}
    meet((up, down, left, right))

    def push(i, src, dst, peer):
        copy = pltpu.make_async_remote_copy(
            src_ref=src, dst_ref=dst, send_sem=send.at[i], recv_sem=recv.at[i],
            device_id=peer, device_id_type=MESH,
        )
        copy.start()
        return copy

    pending = []
    rows = []
    for a, (own, row, col) in enumerate(((nb, nrow, ncol), (gb, grow, gcol))):
        base = 8 * a
        to_up = push(base, own, row.at[1], up)
        to_down = push(base + 1, own, row.at[0], down)
        rows.append((to_down, to_up))
        pending.append(push(base + 2, own.at[0], col.at[0, 1], left))
        pending.append(push(base + 3, own.at[1], col.at[1, 1], right))
    pending.append(push(16, nt, ntp, partner))
    for a, (row, col) in enumerate(((nrow, ncol), (grow, gcol))):
        base = 8 * a + 4
        for side in range(2):
            rows[a][side].wait_recv()
            pending.append(push(base + 2 * side, row.at[side, 0], col.at[0, 2 * side], left))
            pending.append(push(base + 2 * side + 1, row.at[side, 1], col.at[1, 2 * side], right))
    for pair in rows:
        for copy in pair:
            copy.wait_send()
    for copy in pending:
        copy.wait()


def halo_call(nb, gb, nt):
    row = jax.ShapeDtypeStruct((2, 2, INSIDE, D), BF16)
    col = jax.ShapeDtypeStruct((2, 3, INSIDE, D), BF16)
    return pl.pallas_call(
        halo_kernel,
        out_shape=(row, col, row, col, jax.ShapeDtypeStruct((D, OWN), BF16)),
        in_specs=[ANY] * 3,
        out_specs=(ANY,) * 5,
        scratch_shapes=[pltpu.SemaphoreType.DMA((17,)), pltpu.SemaphoreType.DMA((17,))],
        compiler_params=pltpu.CompilerParams(collective_id=0, has_side_effects=True),
        name="halo",
    )(nb, gb, nt)


def assemble(dst, own, row, col):
    for r in range(3):
        base = 4 * INSIDE * r
        middle = own[...] if r == 1 else row[r // 2]
        dst[base : base + OWN, :] = middle.reshape(OWN, middle.shape[-1])
        dst[base + OWN : base + OWN + INSIDE, :] = col[0, r]
        dst[base + OWN + INSIDE : base + 2 * OWN, :] = col[1, r]


def head_lanes(shape):
    return lax.broadcasted_iota(jnp.int32, shape, 1) // HD


def spread_heads(block):
    lanes = head_lanes(block.shape)
    zero = jnp.zeros_like(block)
    return jnp.concatenate([jnp.where(lanes == h, block, zero) for h in range(GROUP)], axis=0)


def pick_heads(stacked):
    lanes = head_lanes((OWN, GW))
    out = stacked[:OWN]
    for h in range(1, GROUP):
        out = jnp.where(lanes == h, stacked[OWN * h : OWN * (h + 1)], out)
    return out


def dot(a, b):
    return lax.dot_general(a, b, (((1,), (0,)), ((), ())), preferred_element_type=F32)


def dot_t(a, b):
    return lax.dot_general(a, b, (((1,), (1,)), ((), ())), preferred_element_type=F32)


def attend_kernel(
    mask_ref, nb, nrow, ncol, wq, wk, wv, gb, fields_ref,
    out_ref, dq_ref, q_ref, k_ref, v_ref, stats_ref,
    n_ext, s_buf, dp_buf, w_buf, ds_buf,
):
    g = pl.program_id(0)

    @pl.when(g == 0)
    def _():
        assemble(n_ext, nb, nrow, ncol)
        lane = lax.broadcasted_iota(jnp.int32, (1, OWN), 1)
        for j in range(8):
            row = jnp.where(lane < INSIDE, mask_ref[0, j], mask_ref[1, j])
            stats_ref[32 + j : 33 + j, :] = row.astype(F32)

    n = n_ext[...]
    q4 = dot(n, wq[...]).astype(BF16)
    k4 = dot(n, wk[...]).astype(BF16)
    v4 = dot(n, wv[...]).astype(BF16)
    q_ref[...] = q4
    mine = slice(4 * INSIDE, 4 * INSIDE + OWN)
    k_ref[...] = k4[mine]
    v_ref[...] = v4[mine]
    grad = gb[...].reshape(OWN, GW)
    s_buf[...] = dot_t(spread_heads(q4[mine]), k4)
    dp_buf[...] = dot_t(spread_heads(grad), v4)

    place = lax.broadcasted_iota(jnp.int32, (1, EXT), 1) // INSIDE
    masks = []
    for b in range(2):
        allowed = jnp.zeros((1, EXT), jnp.int32)
        for r in range(3):
            for p in range(4):
                c = COLUMN_OF[p] - b
                if c < 0 or c > 2:
                    continue
                m = 3 * r + c
                value = 1 if m == 4 else mask_ref[b, m if m < 4 else m - 1]
                allowed = jnp.where(place == 4 * r + p, value, allowed)
        masks.append(jnp.broadcast_to(allowed, (INSIDE, EXT)))
    allowed = jnp.concatenate(masks, axis=0) > 0

    lane = lax.broadcasted_iota(jnp.int32, (OWN, OWN), 1)
    stat = jnp.zeros((OWN, OWN), F32)
    for h in range(GROUP):
        part = slice(OWN * h, OWN * (h + 1))
        s = jnp.where(allowed, s_buf[part, :] * SCALE, NEG_BIG)
        top = jnp.max(s, axis=1, keepdims=True)
        e = jnp.exp(s - top)
        total = jnp.sum(e, axis=1, keepdims=True)
        p = e * (1.0 / total)
        w_buf[part, :] = p.astype(BF16)
        dp = dp_buf[part, :]
        inner = jnp.sum(p * dp, axis=1, keepdims=True)
        ds_buf[part, :] = (p * (dp - inner) * SCALE).astype(BF16)
        stat = jnp.where(lane == h, top + jnp.log(total), stat)
        stat = jnp.where(lane == GROUP + h, inner, stat)
    stats_ref[pl.ds(pl.multiple_of(8 * g, 8), 8), :] = jnp.transpose(stat)[0:8]

    mixed = pick_heads(dot(w_buf[...], v4)).astype(BF16).astype(F32)
    dq_ref[...] = pick_heads(dot(ds_buf[...], k4)).astype(BF16)
    out_ref[...] = (fields_ref[...].astype(F32) + tile_of(mixed)).astype(BF16)


def attend_call(mask, nb, nrow, ncol, w, gb, fields):
    fixed3 = pl.BlockSpec((2, INSIDE, D), lambda g: (0, 0, 0), pipeline_mode=pl.Buffered(1))
    return pl.pallas_call(
        attend_kernel,
        grid=(HEADS // GROUP,),
        out_shape=(
            jax.ShapeDtypeStruct(fields.shape, BF16),
            jax.ShapeDtypeStruct((OWN, D), BF16),
            jax.ShapeDtypeStruct((EXT, D), BF16),
            jax.ShapeDtypeStruct((OWN, D), BF16),
            jax.ShapeDtypeStruct((OWN, D), BF16),
            jax.ShapeDtypeStruct((40, OWN), F32),
        ),
        in_specs=[
            pl.BlockSpec(memory_space=pltpu.SMEM),
            fixed3,
            pl.BlockSpec((2, 2, INSIDE, D), lambda g: (0, 0, 0, 0), pipeline_mode=pl.Buffered(1)),
            pl.BlockSpec((2, 3, INSIDE, D), lambda g: (0, 0, 0, 0), pipeline_mode=pl.Buffered(1)),
            pl.BlockSpec((D, GW), lambda g: (0, g)),
            pl.BlockSpec((D, GW), lambda g: (0, g + 4)),
            pl.BlockSpec((D, GW), lambda g: (0, g + 8)),
            pl.BlockSpec((2, INSIDE, GW), lambda g: (0, 0, g)),
            pl.BlockSpec((BRICK, 2 * BRICK, GW), lambda g: (0, 0, g)),
        ],
        out_specs=(
            pl.BlockSpec((BRICK, 2 * BRICK, GW), lambda g: (0, 0, g)),
            pl.BlockSpec((OWN, GW), lambda g: (0, g)),
            pl.BlockSpec((EXT, GW), lambda g: (0, g)),
            pl.BlockSpec((OWN, GW), lambda g: (0, g)),
            pl.BlockSpec((OWN, GW), lambda g: (0, g)),
            pl.BlockSpec((40, OWN), lambda g: (0, 0)),
        ),
        scratch_shapes=[
            pltpu.VMEM((EXT, D), BF16),
            pltpu.VMEM((GROUP * OWN, EXT), F32),
            pltpu.VMEM((GROUP * OWN, EXT), F32),
            pltpu.VMEM((GROUP * OWN, EXT), BF16),
            pltpu.VMEM((GROUP * OWN, EXT), BF16),
        ],
        compiler_params=pltpu.CompilerParams(vmem_limit_bytes=VMEM_LIMIT),
        name="attend",
    )(mask, nb, nrow, ncol, w, w, w, gb, fields)


def stats_kernel(own, ext, send, recv):
    gx, gy = lax.axis_index("gx"), lax.axis_index("gy")
    spots = [i for i in range(9) if i != 4]
    peers = [shifted(gx, gy, i // 3 - 1, i % 3 - 1) for i in spots]
    meet(peers)
    copies = []
    for i, peer in zip(spots, peers):
        copy = pltpu.make_async_remote_copy(
            src_ref=own, dst_ref=ext.at[8 - i], send_sem=send.at[i], recv_sem=recv.at[i],
            device_id=peer, device_id_type=MESH,
        )
        copy.start()
        copies.append(copy)
    for copy in copies:
        copy.wait()


def stats_call(stats):
    return pl.pallas_call(
        stats_kernel,
        out_shape=jax.ShapeDtypeStruct((9, 40, OWN), F32),
        in_specs=[ANY],
        out_specs=ANY,
        scratch_shapes=[pltpu.SemaphoreType.DMA((9,)), pltpu.SemaphoreType.DMA((9,))],
        compiler_params=pltpu.CompilerParams(collective_id=1, has_side_effects=True),
        name="stats",
    )(stats)


def keys_kernel(
    stats, st_ext, q_ref, k_ref, v_ref, gb, grow, gcol, dq_ref, wq, wk, wv,
    fields_ref, grad_ref, gain_ref,
    dk_ref, dv_ref, gin_ref, ggain_ref,
    g_ext, s_buf, dp_buf, w_buf, ds_buf, gn_buf,
):
    g = pl.program_id(0)
    assemble(g_ext, gb, grow, gcol)
    q4 = q_ref[...]
    g4 = g_ext[...]
    s_buf[...] = dot_t(spread_heads(k_ref[...]), q4)
    dp_buf[...] = dot_t(spread_heads(v_ref[...]), g4)

    def lanes_of(first):
        low = lax.broadcasted_iota(jnp.int32, (8, OWN), 1) < INSIDE
        parts = []
        for r in range(3):
            rows = pl.ds(first, 8)
            middle = stats[rows, :] if r == 1 else st_ext[3 * r + 1, rows, :]
            parts += [middle, jnp.where(low, st_ext[3 * r + 2, rows, :], st_ext[3 * r, rows, :])]
        return jnp.concatenate(parts, axis=1)

    stat = lanes_of(pl.multiple_of(8 * g, 8))
    brick_masks = lanes_of(32)
    place = lax.broadcasted_iota(jnp.int32, (1, EXT), 1) // INSIDE
    masks = []
    for b in range(2):
        allowed = jnp.zeros((1, EXT), F32)
        for r in range(3):
            for p in range(4):
                c = b + 2 - COLUMN_OF[p]
                if c < 0 or c > 2:
                    continue
                m = 3 * (2 - r) + c
                if m == 4:
                    value = jnp.ones((1, EXT), F32)
                else:
                    j = m if m < 4 else m - 1
                    value = brick_masks[j : j + 1, :]
                allowed = jnp.where(place == 4 * r + p, value, allowed)
        masks.append(jnp.broadcast_to(allowed, (INSIDE, EXT)))
    allowed = jnp.concatenate(masks, axis=0) > 0.5

    for h in range(GROUP):
        part = slice(OWN * h, OWN * (h + 1))
        s = jnp.where(allowed, s_buf[part, :] * SCALE - stat[h : h + 1, :], NEG_BIG)
        p = jnp.exp(s)
        w_buf[part, :] = p.astype(BF16)
        inner = stat[GROUP + h : GROUP + h + 1, :]
        ds_buf[part, :] = (p * (dp_buf[part, :] - inner) * SCALE).astype(BF16)

    dv = pick_heads(dot(w_buf[...], g4)).astype(BF16)
    dk = pick_heads(dot(ds_buf[...], q4)).astype(BF16)
    dk_ref[...] = dk
    dv_ref[...] = dv
    step = dot_t(dq_ref[...], wq[...]) + dot_t(dk, wk[...]) + dot_t(dv, wv[...])

    @pl.when(g == 0)
    def _():
        gn_buf[...] = step

    @pl.when(g > 0)
    def _():
        gn_buf[...] += step

    @pl.when(g == HEADS // GROUP - 1)
    def _():
        gn = gn_buf[...]
        x = fields_ref[...].astype(F32)
        x = jnp.concatenate([brick_of(x, 0), brick_of(x, 1)], axis=0)
        inv = lax.rsqrt(jnp.mean(x * x, axis=1, keepdims=True) + EPSILON)
        total = jnp.sum(gn * x * inv, axis=0, keepdims=True)
        for i in range(8):
            ggain_ref[i : i + 1, :] = total[:, 128 * i : 128 * (i + 1)]
        s = gn * gain_ref[...]
        back = inv * (s - x * inv * inv * jnp.mean(s * x, axis=1, keepdims=True))
        gin_ref[...] = (grad_ref[...].astype(F32) + tile_of(back)).astype(BF16)


def keys_call(stats, st_ext, q, k, v, gb, grow, gcol, dq, w, fields, grad_out, gain):
    own = pl.BlockSpec((OWN, GW), lambda g: (0, g))
    tile = pl.BlockSpec((BRICK, 2 * BRICK, D), lambda g: (0, 0, 0), pipeline_mode=pl.Buffered(1))
    return pl.pallas_call(
        keys_kernel,
        grid=(HEADS // GROUP,),
        out_shape=(
            jax.ShapeDtypeStruct((OWN, D), BF16),
            jax.ShapeDtypeStruct((OWN, D), BF16),
            jax.ShapeDtypeStruct(fields.shape, BF16),
            jax.ShapeDtypeStruct((8, 128), F32),
        ),
        in_specs=[
            pl.BlockSpec((40, OWN), lambda g: (0, 0)),
            pl.BlockSpec((9, 40, OWN), lambda g: (0, 0, 0)),
            pl.BlockSpec((EXT, GW), lambda g: (0, g)),
            own,
            own,
            pl.BlockSpec((2, INSIDE, GW), lambda g: (0, 0, g)),
            pl.BlockSpec((2, 2, INSIDE, GW), lambda g: (0, 0, 0, g)),
            pl.BlockSpec((2, 3, INSIDE, GW), lambda g: (0, 0, 0, g)),
            own,
            pl.BlockSpec((D, GW), lambda g: (0, g)),
            pl.BlockSpec((D, GW), lambda g: (0, g + 4)),
            pl.BlockSpec((D, GW), lambda g: (0, g + 8)),
            tile,
            tile,
            pl.BlockSpec((1, D), lambda g: (0, 0)),
        ],
        out_specs=(
            own,
            own,
            pl.BlockSpec((BRICK, 2 * BRICK, D), lambda g: (0, 0, 0)),
            pl.BlockSpec((8, 128), lambda g: (0, 0)),
        ),
        scratch_shapes=[
            pltpu.VMEM((EXT, GW), BF16),
            pltpu.VMEM((GROUP * OWN, EXT), F32),
            pltpu.VMEM((GROUP * OWN, EXT), F32),
            pltpu.VMEM((GROUP * OWN, EXT), BF16),
            pltpu.VMEM((GROUP * OWN, EXT), BF16),
            pltpu.VMEM((OWN, D), F32),
        ],
        compiler_params=pltpu.CompilerParams(vmem_limit_bytes=VMEM_LIMIT),
        name="keys",
    )(stats, st_ext, q, k, v, gb, grow, gcol, dq, w, w, w, fields, grad_out, gain)


CW = 768


def reduce_kernel(
    dq, dk, dv, nt, ntp, gain,
    out, gout,
    b_recv, w_send, r1, s1, r2, s2, r3, fin, r4,
    h1, t1, h2, t2, h3, t3, h4,
    bs, br, s1s, s1r, s2s, s2r, s3s, s3r, s4s, s4r,
):
    gx, gy = lax.axis_index("gx"), lax.axis_index("gy")
    x = gx // 2
    yi = 2 * lax.rem(gx, 2) + gy // 16
    z = lax.rem(gy, 16) // 2
    core = lax.rem(gy, 2)

    def device(x_, yi_, z_, core_):
        return {"gx": 2 * x_ + yi_ // 2, "gy": 16 * lax.rem(yi_, 2) + 2 * z_ + core_}

    partner = device(x, yi, z, 1 - core)
    x_at = [lax.rem(x + d, 4) for d in range(4)]
    y_at = [lax.rem(yi + d, 4) for d in range(4)]
    z_at = [lax.rem(z + d, 8) for d in range(8)]
    x_peer = [device(x_at[d], yi, z, core) for d in range(4)]
    y_peer = [device(x, y_at[d], z, core) for d in range(4)]
    z_peer = [device(x, yi, z_at[d], core) for d in range(8)]
    meet([partner] + x_peer[1:] + y_peer[1:] + z_peer[1:])

    def push(src, dst, send, recv, peer):
        copy = pltpu.make_async_remote_copy(
            src_ref=src, dst_ref=dst, send_sem=send, recv_sem=recv,
            device_id=peer, device_id_type=MESH,
        )
        copy.start()
        return copy

    sources = (dq, dk, dv)
    first = []
    for colour in range(2):
        for t in range(3):
            cols = pl.ds(pl.multiple_of(512 * (1 - core) + 256 * colour, 256), 256)
            at = CW * colour + 256 * t
            i = 3 * colour + t
            first.append(
                push(sources[t].at[:, cols], b_recv.at[:, at : at + 256], bs.at[i], br.at[i], partner)
            )
    for copy in first:
        copy.wait()

    own_b = []
    for colour in range(2):
        cols = pl.ds(pl.multiple_of(512 * core + 256 * colour, 256), 256)
        own_b.append(jnp.concatenate([ref[:, cols] for ref in sources], axis=1))

    def block(colour, row):
        rows = pl.ds(pl.multiple_of(64 * row, 64), 64)
        return dot(nt[rows, :], own_b[colour]) + dot(
            ntp[rows, :], b_recv[:, CW * colour : CW * (colour + 1)]
        )

    stage1 = []
    for slot, d in enumerate((2, 1, 3)):
        for i in range(4):
            w_send[0, slot, i] = block(0, 4 * x_at[d] + i).astype(BF16)
            w_send[1, slot, i] = block(1, 4 * i + y_at[d]).astype(BF16)
        stage1.append(push(w_send.at[0, slot], r1.at[0, slot], s1s.at[slot], s1r.at[slot], x_peer[d]))
        stage1.append(
            push(w_send.at[1, slot], r1.at[1, slot], s1s.at[3 + slot], s1r.at[3 + slot], y_peer[d])
        )
        stage1.append(push(gain, h1.at[slot], s1s.at[6 + slot], s1r.at[6 + slot], x_peer[d]))
    for copy in stage1:
        copy.wait()

    for i in range(4):
        acc = block(0, 4 * x + i)
        for slot in range(3):
            acc = acc + r1[0, slot, i].astype(F32)
        s1[0, i] = acc.astype(BF16)
        acc = block(1, 4 * i + yi)
        for slot in range(3):
            acc = acc + r1[1, slot, i].astype(F32)
        s1[1, i] = acc.astype(BF16)
    t1[...] = gain[...] + h1[0] + h1[1] + h1[2]

    stage2 = []
    for slot, d in enumerate((2, 1, 3)):
        stage2.append(push(s1.at[0, y_at[d]], r2.at[0, slot], s2s.at[slot], s2r.at[slot], y_peer[d]))
        stage2.append(
            push(s1.at[1, x_at[d]], r2.at[1, slot], s2s.at[3 + slot], s2r.at[3 + slot], x_peer[d])
        )
        stage2.append(push(t1, h2.at[slot], s2s.at[6 + slot], s2r.at[6 + slot], y_peer[d]))
    for copy in stage2:
        copy.wait()

    for colour, mine in ((0, yi), (1, x)):
        acc = s1[colour, mine].astype(F32)
        for slot in range(3):
            acc = acc + r2[colour, slot].astype(F32)
        for zz in range(8):
            s2[zz, :, CW * colour : CW * (colour + 1)] = acc[8 * zz : 8 * zz + 8].astype(BF16)
    t2[...] = t1[...] + h2[0] + h2[1] + h2[2]

    stage3 = []
    for slot, d in enumerate((4, 3, 5, 2, 6, 1, 7)):
        stage3.append(push(s2.at[z_at[d]], r3.at[slot], s3s.at[slot], s3r.at[slot], z_peer[d]))
        stage3.append(push(t2, h3.at[slot], s3s.at[7 + slot], s3r.at[7 + slot], z_peer[d]))
    for copy in stage3:
        copy.wait()

    acc = s2[z].astype(F32)
    tot = t2[...]
    for slot in range(7):
        acc = acc + r3[slot].astype(F32)
        tot = tot + h3[slot]
    t3[...] = tot
    acc = acc * (ALL_TOKENS ** (-0.5))
    fin[0] = acc[0:4]
    fin[1] = acc[4:8]
    last = [
        push(fin.at[1 - core], r4, s4s.at[0], s4r.at[0], partner),
        push(t3, h4, s4s.at[1], s4r.at[1], partner),
    ]
    for copy in last:
        copy.wait()
    gout[...] = (t3[...] + h4[...]) * (ALL_TOKENS ** (-0.5))
    mine, other = fin[core], r4[...]
    is_first = jnp.broadcast_to(core, mine.shape) == 0
    halves = (jnp.where(is_first, mine, other), jnp.where(is_first, other, mine))
    for t in range(3):
        for half in range(2):
            for colour in range(2):
                to = 1024 * t + 512 * half + 256 * colour
                at = CW * colour + 256 * t
                out[:, to : to + 256] = halves[half][:, at : at + 256]


def reduce_call(dq, dk, dv, nt, ntp, gain):
    dma = pltpu.SemaphoreType.DMA
    tile = (8, 128)
    return pl.pallas_call(
        reduce_kernel,
        out_shape=(jax.ShapeDtypeStruct((4, 3 * D), F32), jax.ShapeDtypeStruct(tile, F32)),
        in_specs=[VM] * 6,
        out_specs=(VM, VM),
        scratch_shapes=[
            pltpu.VMEM((OWN, 2 * CW), BF16),
            pltpu.VMEM((2, 3, 4, 64, CW), BF16),
            pltpu.VMEM((2, 3, 4, 64, CW), BF16),
            pltpu.VMEM((2, 4, 64, CW), BF16),
            pltpu.VMEM((2, 3, 64, CW), BF16),
            pltpu.VMEM((8, 8, 2 * CW), BF16),
            pltpu.VMEM((7, 8, 2 * CW), BF16),
            pltpu.VMEM((2, 4, 2 * CW), F32),
            pltpu.VMEM((4, 2 * CW), F32),
            pltpu.VMEM((3,) + tile, F32),
            pltpu.VMEM(tile, F32),
            pltpu.VMEM((3,) + tile, F32),
            pltpu.VMEM(tile, F32),
            pltpu.VMEM((7,) + tile, F32),
            pltpu.VMEM(tile, F32),
            pltpu.VMEM(tile, F32),
            dma((6,)), dma((6,)),
            dma((9,)), dma((9,)),
            dma((9,)), dma((9,)),
            dma((14,)), dma((14,)),
            dma((2,)), dma((2,)),
        ],
        compiler_params=pltpu.CompilerParams(
            collective_id=2, has_side_effects=True, vmem_limit_bytes=VMEM_LIMIT
        ),
        name="reduce",
    )(dq, dk, dv, nt, ntp, gain)


def per_device(fields, grad_out, norm_gain, w_qkv, brick_mask):
    gain = norm_gain.reshape(1, D)
    mask = brick_mask.reshape(2, 8)
    nb, nt, gb = norm_call(fields, grad_out, gain)
    nrow, ncol, grow, gcol, ntp = halo_call(nb, gb, nt)
    output, dq, q, k, v, stats = attend_call(mask, nb, nrow, ncol, w_qkv, gb, fields)
    st_ext = stats_call(stats)
    dk, dv, grad_in, ggain = keys_call(
        stats, st_ext, q, k, v, gb, grow, gcol, dq, w_qkv, fields, grad_out, gain
    )
    w_grad, gain_sum = reduce_call(dq, dk, dv, nt, ntp, ggain)
    owner = lax.axis_index("gx") * lax.axis_size("gy") + lax.axis_index("gy")
    gain_grad = lax.dynamic_slice(gain_sum.reshape(D), (4 * owner,), (4,))
    return (output, grad_in, w_grad, gain_grad)


def solution(mesh):
    placed = (P("gx", "gy", None), P("gx", "gy", None), P(), P(), P("gx", "gy", None))
    return jax.shard_map(
        per_device,
        mesh=mesh,
        in_specs=placed,
        out_specs=(
            P("gx", "gy", None),
            P("gx", "gy", None),
            P(("gx", "gy"), None),
            P(("gx", "gy")),
        ),
        check_vma=False,
    )
```

```python
import jax
import jax.numpy as jnp
from jax import lax
from jax.experimental import pallas as pl
from jax.experimental.pallas import tpu as pltpu
from jax.sharding import PartitionSpec as P

HEADS = 16
BRICK = 8
D = 1024
HD = 64
GROUP = 4
GW = GROUP * HD
INSIDE = BRICK * BRICK
OWN = 2 * INSIDE
EXT = 12 * INSIDE
EPSILON = 1e-05
NEG_BIG = -1e30
SCALE = HD ** (-0.5)
ALL_TOKENS = 32768
MESH = pl.DeviceIdType.MESH
F32 = jnp.float32
BF16 = jnp.bfloat16
ANY = pl.BlockSpec(memory_space=pl.ANY)
VM = pl.BlockSpec(memory_space=pltpu.VMEM)
SM = pl.BlockSpec(memory_space=pltpu.SMEM)
VMEM_LIMIT = 56 * 1024 * 1024

COLUMN_OF = (1, 2, 3, 0)


def brick_of(tile, b):
    part = tile[:, BRICK * b : BRICK * (b + 1), :]
    return part.reshape(INSIDE, part.shape[-1])


def tile_of(bricks):
    width = bricks.shape[-1]
    first = bricks[:INSIDE].reshape(BRICK, BRICK, width)
    second = bricks[INSIDE:].reshape(BRICK, BRICK, width)
    return jnp.concatenate([first, second], axis=1)


def shifted(gx, gy, dx, dy):
    nx, ny = lax.axis_size("gx"), lax.axis_size("gy")
    return {"gx": lax.rem(gx + dx + nx, nx), "gy": lax.rem(gy + dy + ny, ny)}


def dot(a, b):
    return lax.dot_general(a, b, (((1,), (0,)), ((), ())), preferred_element_type=F32)


def dot_t(a, b):
    return lax.dot_general(a, b, (((1,), (1,)), ((), ())), preferred_element_type=F32)


def head_lanes(shape):
    return lax.broadcasted_iota(jnp.int32, shape, 1) // HD


def spread_heads(block):
    lanes = head_lanes(block.shape)
    zero = jnp.zeros_like(block)
    return jnp.concatenate([jnp.where(lanes == h, block, zero) for h in range(GROUP)], axis=0)


def pick_heads(stacked):
    lanes = head_lanes((OWN, GW))
    out = stacked[:OWN]
    for h in range(1, GROUP):
        out = jnp.where(lanes == h, stacked[OWN * h : OWN * (h + 1)], out)
    return out


def bricks_of(tile):
    return jnp.concatenate([brick_of(tile, 0), brick_of(tile, 1)], axis=0)


def at(index, size):
    start = index * size
    return pl.ds(start if isinstance(start, int) else pl.multiple_of(start, size), size)


def steps(first, last, body):
    if UNROLL:
        for g in range(first, last):
            body(g)
    else:

        def once(g, carry):
            body(g)
            return carry

        lax.fori_loop(first, last, once, 0)


UNROLL = False
GROUPS = HEADS // GROUP
HW = GW // 2
CW = 3 * HW
SPOTS = (0, 1, 2, 3, 5, 6, 7, 8)
PLACE = 4 * INSIDE
MINE = slice(PLACE, PLACE + OWN)
HALO, STAT, PAIR, ONE, TWO, THREE, FOUR, SEMS = 0, 17, 62, 66, 93, 120, 134, 136


def layer_kernel(
    mask_ref, fields_ref, grad_ref, gain_ref, w_hbm,
    out_ref, gin_ref, wg_ref, gg_ref,
    w, n_ext, g_ext, a2, q_ext, k_ext, v_ext, dq_all, dk_all, dv_all,
    s_buf, dp_buf, w_buf, ds_buf, stats, st_ext,
    b_own, b_other, w_send, r1, s1, r2, s2, r3, fin, r4,
    h0, h1, t1, h2, t2, h3, t3, h4,
    load_sem, send, recv,
):
    gx, gy = lax.axis_index("gx"), lax.axis_index("gy")
    up, down = shifted(gx, gy, -1, 0), shifted(gx, gy, 1, 0)
    left, right = shifted(gx, gy, 0, -1), shifted(gx, gy, 0, 1)
    around = [shifted(gx, gy, i // 3 - 1, i % 3 - 1) for i in SPOTS]
    x, yi = gx // 2, 2 * lax.rem(gx, 2) + gy // 16
    z, core = lax.rem(gy, 16) // 2, lax.rem(gy, 2)

    def device(x_, yi_, z_, core_):
        return {"gx": 2 * x_ + yi_ // 2, "gy": 16 * lax.rem(yi_, 2) + 2 * z_ + core_}

    partner = device(x, yi, z, 1 - core)
    x_at = [lax.rem(x + d, 4) for d in range(4)]
    y_at = [lax.rem(yi + d, 4) for d in range(4)]
    z_at = [lax.rem(z + d, 8) for d in range(8)]
    x_peer = [device(x_at[d], yi, z, core) for d in range(4)]
    y_peer = [device(x, y_at[d], z, core) for d in range(4)]
    z_peer = [device(x, yi, z_at[d], core) for d in range(8)]

    def copy_of(i, src, dst, peer):
        return pltpu.make_async_remote_copy(
            src_ref=src, dst_ref=dst, send_sem=send.at[i], recv_sem=recv.at[i],
            device_id=peer, device_id_type=MESH,
        )

    sent = []

    def push(i, src, dst, peer):
        copy = copy_of(i, src, dst, peer)
        copy.start()
        sent.append(copy)
        return copy

    loads = [
        pltpu.make_async_copy(w_hbm.at[:, at(t, D)], w.at[:, at(t, D)], load_sem.at[t])
        for t in range(3)
    ]
    for load in loads:
        load.start()

    peers = around + x_peer[1:] + y_peer[1:] + z_peer[1:]
    barrier = pltpu.get_barrier_semaphore()
    for peer in peers:
        pl.semaphore_signal(barrier, inc=1, device_id=peer, device_id_type=MESH)

    xf = bricks_of(fields_ref[...].astype(F32))
    inv = lax.rsqrt(jnp.mean(xf * xf, axis=1, keepdims=True) + EPSILON)
    n = (xf * inv * gain_ref[...]).astype(BF16)
    n_ext[1, 0:2] = n.reshape(2, INSIDE, D)
    a2[0] = jnp.transpose(n.astype(F32)).astype(BF16)
    g_ext[1, 0:2] = bricks_of(grad_ref[...].astype(F32)).astype(BF16).reshape(2, INSIDE, D)
    lane = lax.broadcasted_iota(jnp.int32, (1, OWN), 1)
    for j in range(8):
        row = jnp.where(lane < INSIDE, mask_ref[0, j], mask_ref[1, j])
        stats[32 + j : 33 + j, :] = row.astype(F32)
    pl.semaphore_wait(barrier, len(peers))

    def send_rows(base, ext):
        to_up = push(base, ext.at[1, 0:2], ext.at[2, 0:2], up)
        to_down = push(base + 1, ext.at[1, 0:2], ext.at[0, 0:2], down)
        return [
            (to_down, to_up),
            push(base + 2, ext.at[1, 0], ext.at[1, 2], left),
            push(base + 3, ext.at[1, 1], ext.at[1, 3], right),
        ]

    def send_corners(base, ext, pair):
        out = []
        for side in range(2):
            r = 2 * side
            pair[side].wait_recv()
            out.append(push(base + 4 + r, ext.at[r, 0], ext.at[r, 2], left))
            out.append(push(base + 5 + r, ext.at[r, 1], ext.at[r, 3], right))
        return out

    def stat_copy(i, g, peer):
        rows = at(g, 8)
        return copy_of(STAT + 9 * g + i, stats.at[rows, :], st_ext.at[8 - i, rows, :], peer)

    n_pair, *n_cols = send_rows(HALO, n_ext)
    a2_copy = push(16, a2.at[0], a2.at[1], partner)
    for i, peer in zip(SPOTS, around):
        stat_copy(i, GROUPS, peer).start()

    def project(rows, targets):
        def one(j):
            for t, dst in enumerate((q_ext, k_ext, v_ext)):
                part = pl.ds(pl.multiple_of(D * t + GW * j, GW), GW)
                made = dot(rows, w[:, part]).astype(BF16)
                for i, to in enumerate(targets):
                    dst[to : to + OWN, at(j, GW)] = made[OWN * i : OWN * (i + 1)]

        def once(j, carry):
            one(j)
            return carry

        lax.fori_loop(0, GROUPS, once, 0)

    for load in loads:
        load.wait()
    project(n_ext[1, 0:2].reshape(OWN, D), (PLACE,))
    n_cols += send_corners(HALO, n_ext, n_pair)
    g_pair, *g_cols = send_rows(HALO + 8, g_ext)
    project(
        jnp.concatenate([n_ext[r, 0:2].reshape(OWN, D) for r in (0, 2)], axis=0), (0, 2 * PLACE)
    )
    for copy in n_cols:
        copy.wait_recv()
    project(
        jnp.concatenate([n_ext[r, 2:4].reshape(OWN, D) for r in range(3)], axis=0),
        (OWN, PLACE + OWN, 2 * PLACE + OWN),
    )

    place = lax.broadcasted_iota(jnp.int32, (1, EXT), 1) // INSIDE

    def attend(g):
        cols = at(g, GW)
        k4, v4 = k_ext[:, cols], v_ext[:, cols]
        s_buf[...] = dot_t(spread_heads(q_ext[MINE, cols]), k4)
        dp_buf[...] = dot_t(spread_heads(g_ext[1, 0:2, :, cols].reshape(OWN, GW)), v4)
        masks = []
        for b in range(2):
            allowed = jnp.zeros((1, EXT), jnp.int32)
            for r in range(3):
                for p in range(4):
                    c = COLUMN_OF[p] - b
                    if c < 0 or c > 2:
                        continue
                    m = 3 * r + c
                    value = 1 if m == 4 else mask_ref[b, m if m < 4 else m - 1]
                    allowed = jnp.where(place == 4 * r + p, value, allowed)
            masks.append(jnp.broadcast_to(allowed, (INSIDE, EXT)))
        allowed = jnp.concatenate(masks, axis=0) > 0
        lane = lax.broadcasted_iota(jnp.int32, (OWN, OWN), 1)
        stat = jnp.zeros((OWN, OWN), F32)
        for h in range(GROUP):
            part = slice(OWN * h, OWN * (h + 1))
            s = jnp.where(allowed, s_buf[part, :] * SCALE, NEG_BIG)
            top = jnp.max(s, axis=1, keepdims=True)
            e = jnp.exp(s - top)
            total = jnp.sum(e, axis=1, keepdims=True)
            p = e * (1.0 / total)
            w_buf[part, :] = p.astype(BF16)
            dp = dp_buf[part, :]
            inner = jnp.sum(p * dp, axis=1, keepdims=True)
            ds_buf[part, :] = (p * (dp - inner) * SCALE).astype(BF16)
            stat = jnp.where(lane == h, top + jnp.log(total), stat)
            stat = jnp.where(lane == GROUP + h, inner, stat)
        stats[at(g, 8), :] = jnp.transpose(stat)[0:8]
        for i, peer in zip(SPOTS, around):
            stat_copy(i, g, peer).start()
        mixed = pick_heads(dot(w_buf[...], v4)).astype(BF16).astype(F32)
        dq_all[:, cols] = pick_heads(dot(ds_buf[...], k4)).astype(BF16)
        out_ref[:, :, cols] = (fields_ref[:, :, cols].astype(F32) + tile_of(mixed)).astype(BF16)

    steps(0, 2, attend)
    g_cols += send_corners(HALO + 8, g_ext, g_pair)
    steps(2, GROUPS, attend)

    for copy in g_cols + [a2_copy]:
        copy.wait_recv()
    for i, peer in zip(SPOTS, around):
        stat_copy(i, GROUPS, peer).wait()

    def lanes_of(g):
        low = lax.broadcasted_iota(jnp.int32, (8, OWN), 1) < INSIDE
        rows = at(g, 8)
        parts = []
        for r in range(3):
            middle = stats[rows, :] if r == 1 else st_ext[3 * r + 1, rows, :]
            parts += [middle, jnp.where(low, st_ext[3 * r + 2, rows, :], st_ext[3 * r, rows, :])]
        return jnp.concatenate(parts, axis=1)

    def pair_copy(g):
        return copy_of(PAIR + g, b_own.at[g, 1 - core], b_other.at[g], partner)

    def one_copies(g):
        out = []
        for slot, d in enumerate((2, 1, 3)):
            base = ONE + 6 * g + slot
            out.append(copy_of(base, w_send.at[g, x_at[d], :, 0], r1.at[g, 0, slot], x_peer[d]))
            out.append(copy_of(base + 3, w_send.at[g, :, y_at[d], 1], r1.at[g, 1, slot], y_peer[d]))
        return out

    def weigh(g):
        pair_copy(g).wait()
        both = jnp.concatenate([b_own[g, core], b_other[g]], axis=0)
        for part in range(4):
            rows = slice(256 * part, 256 * (part + 1))
            left_side = jnp.concatenate([a2[0, rows, :], a2[1, rows, :]], axis=1)
            w_send[g, part] = dot(left_side, both).astype(BF16).reshape(4, 2, 32, CW)
        for copy in one_copies(g):
            copy.start()

    def keys(g):
        cols = at(g, GW)
        for i, peer in zip(SPOTS, around):
            stat_copy(i, g, peer).wait()
        q4 = q_ext[:, cols]
        g4 = g_ext[:, :, :, cols].reshape(EXT, GW)
        s_buf[...] = dot_t(spread_heads(k_ext[MINE, cols]), q4)
        dp_buf[...] = dot_t(spread_heads(v_ext[MINE, cols]), g4)
        stat, brick_masks = lanes_of(g), lanes_of(GROUPS)
        masks = []
        for b in range(2):
            allowed = jnp.zeros((1, EXT), F32)
            for r in range(3):
                for p in range(4):
                    c = b + 2 - COLUMN_OF[p]
                    if c < 0 or c > 2:
                        continue
                    m = 3 * (2 - r) + c
                    j = m if m < 4 else m - 1
                    value = jnp.ones((1, EXT), F32) if m == 4 else brick_masks[j : j + 1, :]
                    allowed = jnp.where(place == 4 * r + p, value, allowed)
            masks.append(jnp.broadcast_to(allowed, (INSIDE, EXT)))
        allowed = jnp.concatenate(masks, axis=0) > 0.5
        for h in range(GROUP):
            part = slice(OWN * h, OWN * (h + 1))
            s = jnp.where(allowed, s_buf[part, :] * SCALE - stat[h : h + 1, :], NEG_BIG)
            p = jnp.exp(s)
            w_buf[part, :] = p.astype(BF16)
            inner = stat[GROUP + h : GROUP + h + 1, :]
            ds_buf[part, :] = (p * (dp_buf[part, :] - inner) * SCALE).astype(BF16)
        dv4 = pick_heads(dot(w_buf[...], g4)).astype(BF16)
        dk4 = pick_heads(dot(ds_buf[...], q4)).astype(BF16)
        dk_all[:, cols] = dk4
        dv_all[:, cols] = dv4
        dq4 = dq_all[:, cols]
        for half in range(2):
            b_own[g, half] = jnp.concatenate(
                [value[:, HW * half : HW * (half + 1)] for value in (dq4, dk4, dv4)], axis=1
            )
        pair_copy(g).start()
        if isinstance(g, int):
            if g > 0:
                weigh(g - 1)
        else:
            pl.when(g > 0)(lambda: weigh(g - 1))

    steps(0, GROUPS, keys)
    weigh(GROUPS - 1)

    grads = (dq_all[...], dk_all[...], dv_all[...])
    parts = []
    for j in range(4):
        rows = at(j, GW)
        made = dot_t(grads[0], w[rows, 0:D])
        made = made + dot_t(grads[1], w[rows, D : 2 * D])
        parts.append(made + dot_t(grads[2], w[rows, 2 * D : 3 * D]))
    gn = jnp.concatenate(parts, axis=1)
    xf = bricks_of(fields_ref[...].astype(F32))
    inv = lax.rsqrt(jnp.mean(xf * xf, axis=1, keepdims=True) + EPSILON)
    total = jnp.sum(gn * xf * inv, axis=0, keepdims=True)
    for i in range(8):
        h0[i : i + 1, :] = total[:, 128 * i : 128 * (i + 1)]
    for slot, d in enumerate((2, 1, 3)):
        push(ONE + 24 + slot, h0, h1.at[slot], x_peer[d])
    s = gn * gain_ref[...]
    back = inv * (s - xf * inv * inv * jnp.mean(s * xf, axis=1, keepdims=True))
    gin_ref[...] = (grad_ref[...].astype(F32) + tile_of(back)).astype(BF16)

    two = []
    for g in range(GROUPS):
        for copy in one_copies(g):
            copy.wait()
        for i in range(4):
            acc = w_send[g, x, i, 0].astype(F32)
            for slot in range(3):
                acc = acc + r1[g, 0, slot, i].astype(F32)
            s1[g, 0, i] = acc.astype(BF16)
            acc = w_send[g, i, yi, 1].astype(F32)
            for slot in range(3):
                acc = acc + r1[g, 1, slot, i].astype(F32)
            s1[g, 1, i] = acc.astype(BF16)
        mine = []
        for slot, d in enumerate((2, 1, 3)):
            base = TWO + 6 * g + slot
            mine.append(push(base, s1.at[g, 0, y_at[d]], r2.at[g, 0, slot], y_peer[d]))
            mine.append(push(base + 3, s1.at[g, 1, x_at[d]], r2.at[g, 1, slot], x_peer[d]))
        two.append(mine)

    gains = [copy_of(ONE + 24 + slot, h0, h1.at[slot], x_peer[1]) for slot in range(3)]
    for copy in gains:
        copy.wait_recv()
    t1[...] = h0[...] + h1[0] + h1[1] + h1[2]
    gains = []
    for slot, d in enumerate((2, 1, 3)):
        gains.append(push(TWO + 24 + slot, t1, h2.at[slot], y_peer[d]))

    for g in range(GROUPS):
        for copy in two[g]:
            copy.wait_recv()
        for colour, mine in ((0, yi), (1, x)):
            acc = s1[g, colour, mine].astype(F32)
            for slot in range(3):
                acc = acc + r2[g, colour, slot].astype(F32)
            for zz in range(4):
                s2[4 * colour + zz, :, CW * g : CW * (g + 1)] = acc[8 * zz : 8 * zz + 8].astype(BF16)
    for copy in gains:
        copy.wait_recv()
    t2[...] = t1[...] + h2[0] + h2[1] + h2[2]

    three = []
    for slot, d in enumerate((4, 3, 5, 2, 6, 1, 7)):
        three.append(push(THREE + slot, s2.at[z_at[d]], r3.at[slot], z_peer[d]))
        three.append(push(THREE + 7 + slot, t2, h3.at[slot], z_peer[d]))
    for copy in three:
        copy.wait_recv()
    acc = s2[z].astype(F32)
    tot = t2[...]
    for slot in range(7):
        acc = acc + r3[slot].astype(F32)
        tot = tot + h3[slot]
    t3[...] = tot
    acc = acc * (ALL_TOKENS ** (-0.5))
    fin[0] = acc[0:4]
    fin[1] = acc[4:8]
    four = [push(FOUR, fin.at[1 - core], r4, partner), push(FOUR + 1, t3, h4, partner)]
    for copy in four:
        copy.wait_recv()
    gg_ref[...] = (t3[...] + h4[...]) * (ALL_TOKENS ** (-0.5))
    mine, other = fin[core], r4[...]
    is_first = jnp.broadcast_to(core, mine.shape) == 0
    halves = (jnp.where(is_first, mine, other), jnp.where(is_first, other, mine))
    for g in range(GROUPS):
        for t in range(3):
            for half in range(2):
                to = D * t + GW * g + HW * half
                come = CW * g + HW * t
                wg_ref[:, to : to + HW] = halves[half][:, come : come + HW]
    for copy in sent:
        copy.wait_send()


def layer_call(mask, fields, grad_out, gain, w):
    dma = pltpu.SemaphoreType.DMA
    vm = pltpu.VMEM
    tile = (8, 128)
    stack = (GROUP * OWN, EXT)
    return pl.pallas_call(
        layer_kernel,
        out_shape=(
            jax.ShapeDtypeStruct(fields.shape, BF16),
            jax.ShapeDtypeStruct(fields.shape, BF16),
            jax.ShapeDtypeStruct((4, 3 * D), F32),
            jax.ShapeDtypeStruct(tile, F32),
        ),
        in_specs=[SM, VM, VM, VM, ANY],
        out_specs=(VM,) * 4,
        scratch_shapes=[
            vm((D, 3 * D), BF16),
            vm((3, 4, INSIDE, D), BF16), vm((3, 4, INSIDE, D), BF16),
            vm((2, D, OWN), BF16),
            vm((EXT, D), BF16), vm((EXT, D), BF16), vm((EXT, D), BF16),
            vm((OWN, D), BF16), vm((OWN, D), BF16), vm((OWN, D), BF16),
            vm(stack, F32), vm(stack, F32), vm(stack, BF16), vm(stack, BF16),
            vm((40, OWN), F32), vm((9, 40, OWN), F32),
            vm((GROUPS, 2, OWN, CW), BF16), vm((GROUPS, OWN, CW), BF16),
            vm((GROUPS, 4, 4, 2, 32, CW), BF16),
            vm((GROUPS, 2, 3, 4, 32, CW), BF16),
            vm((GROUPS, 2, 4, 32, CW), BF16),
            vm((GROUPS, 2, 3, 32, CW), BF16),
            vm((8, 8, GROUPS * CW), BF16),
            vm((7, 8, GROUPS * CW), BF16),
            vm((2, 4, GROUPS * CW), F32),
            vm((4, GROUPS * CW), F32),
            vm(tile, F32), vm((3,) + tile, F32),
            vm(tile, F32), vm((3,) + tile, F32),
            vm(tile, F32), vm((7,) + tile, F32),
            vm(tile, F32), vm(tile, F32),
            dma((3,)), dma((SEMS,)), dma((SEMS,)),
        ],
        compiler_params=pltpu.CompilerParams(
            collective_id=0, has_side_effects=True, vmem_limit_bytes=VMEM_LIMIT
        ),
        name="layer",
    )(mask, fields, grad_out, gain, w)


def per_device(fields, grad_out, norm_gain, w_qkv, brick_mask):
    output, grad_in, w_grad, gain_sum = layer_call(
        brick_mask.reshape(2, 8), fields, grad_out, norm_gain.reshape(1, D), w_qkv
    )
    owner = lax.axis_index("gx") * lax.axis_size("gy") + lax.axis_index("gy")
    gain_grad = lax.dynamic_slice(gain_sum.reshape(D), (4 * owner,), (4,))
    return (output, grad_in, w_grad, gain_grad)


def solution(mesh):
    placed = (P("gx", "gy", None), P("gx", "gy", None), P(), P(), P("gx", "gy", None))
    return jax.shard_map(
        per_device,
        mesh=mesh,
        in_specs=placed,
        out_specs=(
            P("gx", "gy", None),
            P("gx", "gy", None),
            P(("gx", "gy"), None),
            P(("gx", "gy")),
        ),
        check_vma=False,
    )
```

```python
import jax
import jax.numpy as jnp
from jax import lax
from jax.experimental import pallas as pl
from jax.experimental.pallas import tpu as pltpu
from jax.sharding import PartitionSpec as P

HEADS = 16
BRICK = 8
D = 1024
HD = 64
GROUP = 4
GW = GROUP * HD
INSIDE = BRICK * BRICK
OWN = 2 * INSIDE
EXT = 12 * INSIDE
EPSILON = 1e-05
NEG_BIG = -1e30
SCALE = HD ** (-0.5)
ALL_TOKENS = 32768
MESH = pl.DeviceIdType.MESH
F32 = jnp.float32
BF16 = jnp.bfloat16
ANY = pl.BlockSpec(memory_space=pl.ANY)
VM = pl.BlockSpec(memory_space=pltpu.VMEM)
SM = pl.BlockSpec(memory_space=pltpu.SMEM)
VMEM_LIMIT = 56 * 1024 * 1024

ROW_OF = (1, 0, 2)
COLUMN_OF = (1, 2, 3, 0)


def brick_of(tile, b):
    part = tile[:, BRICK * b : BRICK * (b + 1), :]
    return part.reshape(INSIDE, part.shape[-1])


def tile_of(bricks):
    width = bricks.shape[-1]
    first = bricks[:INSIDE].reshape(BRICK, BRICK, width)
    second = bricks[INSIDE:].reshape(BRICK, BRICK, width)
    return jnp.concatenate([first, second], axis=1)


def shifted(gx, gy, dx, dy):
    nx, ny = lax.axis_size("gx"), lax.axis_size("gy")
    return {"gx": lax.rem(gx + dx + nx, nx), "gy": lax.rem(gy + dy + ny, ny)}


def dot(a, b):
    return lax.dot_general(a, b, (((1,), (0,)), ((), ())), preferred_element_type=F32)


def dot_t(a, b):
    return lax.dot_general(a, b, (((1,), (1,)), ((), ())), preferred_element_type=F32)


def head_lanes(shape):
    return lax.broadcasted_iota(jnp.int32, shape, 1) // HD


def spread_heads(block):
    lanes = head_lanes(block.shape)
    zero = jnp.zeros_like(block)
    return jnp.concatenate([jnp.where(lanes == h, block, zero) for h in range(GROUP)], axis=0)


def pick_heads(stacked):
    lanes = head_lanes((OWN, GW))
    out = stacked[:OWN]
    for h in range(1, GROUP):
        out = jnp.where(lanes == h, stacked[OWN * h : OWN * (h + 1)], out)
    return out


def bricks_of(tile):
    return jnp.concatenate([brick_of(tile, 0), brick_of(tile, 1)], axis=0)


def at(index, size):
    start = index * size
    return pl.ds(start if isinstance(start, int) else pl.multiple_of(start, size), size)


def steps(first, last, body):
    def once(g, carry):
        body(g)
        return carry

    lax.fori_loop(first, last, once, 0)


GROUPS = HEADS // GROUP
HW = GW // 2
UNITS = 6
UW = 2 * HW
SPOTS = (0, 1, 2, 3, 5, 6, 7, 8)
MINE = slice(0, OWN)
SIBLINGS = (2, 1, 3)
FAR_FIRST = (4, 3, 5, 2, 6, 1, 7)
(N_NEAR, N_FAR, N_MID, N_CORNER, G_NEAR, G_FAR, G_MID, G_CORNER, A2, STAT, PAIR, ONE, TWO, THREE,
 FOUR, GAIN, SEMS) = (0, 4, 6, 7, 8, 10, 12, 13, 14, 15, 20, 26, 32, 38, 40, 41, 45)


def layer_kernel(
    mask_ref, fields_ref, grad_ref, gain_ref, w_hbm,
    out_hbm, gin_hbm, wg_ref, gg_ref,
    w, n_ext, g_ext, a2, q_ext, k_ext, v_ext, dq_all, dk_all, dv_all,
    s_buf, dp_buf, w_buf, ds_buf, stats, st_ext, out_v, gin_v,
    b_own, b_other, w_send, r1, s1, r2, s2, r3, fin, r4,
    h0, h1, t1, h2, t2, h3, t3, h4,
    local_sem, send, recv,
):
    gx, gy = lax.axis_index("gx"), lax.axis_index("gy")
    left, right = shifted(gx, gy, 0, -1), shifted(gx, gy, 0, 1)
    around = [shifted(gx, gy, i // 3 - 1, i % 3 - 1) for i in SPOTS]
    odd = lax.rem(gx, 2)
    x, yi = gx // 2, 2 * odd + gy // 16
    z, core = lax.rem(gy, 16) // 2, lax.rem(gy, 2)

    def device(x_, yi_, z_, core_):
        return {"gx": 2 * x_ + yi_ // 2, "gy": 16 * lax.rem(yi_, 2) + 2 * z_ + core_}

    partner = device(x, yi, z, 1 - core)
    x_at = [lax.rem(x + d, 4) for d in range(4)]
    y_at = [lax.rem(yi + d, 4) for d in range(4)]
    z_at = [lax.rem(z + d, 8) for d in range(8)]
    x_peer = [device(x_at[d], yi, z, core) for d in range(4)]
    y_peer = [device(x, y_at[d], z, core) for d in range(4)]
    z_peer = [device(x, yi, z_at[d], core) for d in range(8)]
    mate = {"gx": gx + 1 - 2 * odd, "gy": gy}
    onward = {"gx": lax.rem(gx + 2 + 4 * odd, 8), "gy": gy}
    near, far = 2 - odd, 1 + odd

    def copy_of(i, src, dst, peer):
        return pltpu.make_async_remote_copy(
            src_ref=src, dst_ref=dst, send_sem=send.at[i], recv_sem=recv.at[i],
            device_id=peer, device_id_type=MESH,
        )

    def push(i, src, dst, peer):
        copy_of(i, src, dst, peer).start()

    def arrive(i, ref):
        copy_of(i, ref, ref, partner).wait_recv()

    def leave(i, ref):
        copy_of(i, ref, ref, partner).wait_send()

    loads = [
        pltpu.make_async_copy(w_hbm.at[:, at(t, D)], w.at[:, at(t, D)], local_sem.at[t])
        for t in range(3)
    ]
    for load in loads:
        load.start()

    peers = around + x_peer[1:] + y_peer[1:] + z_peer[1:]
    barrier = pltpu.get_barrier_semaphore()
    for peer in peers:
        pl.semaphore_signal(barrier, inc=1, device_id=peer, device_id_type=MESH)

    xf = bricks_of(fields_ref[...].astype(F32))
    inv = lax.rsqrt(jnp.mean(xf * xf, axis=1, keepdims=True) + EPSILON)
    n = (xf * inv * gain_ref[...]).astype(BF16)
    n_ext[0, 0:2] = n.reshape(2, INSIDE, D)
    a2[0] = jnp.transpose(n.astype(F32)).astype(BF16)
    g_ext[0, 0:2] = bricks_of(grad_ref[...].astype(F32)).astype(BF16).reshape(2, INSIDE, D)
    lane = lax.broadcasted_iota(jnp.int32, (1, OWN), 1)
    for j in range(8):
        row = jnp.where(lane < INSIDE, mask_ref[0, j], mask_ref[1, j])
        stats[GROUPS, j : j + 1, :] = row.astype(F32)
    pl.semaphore_wait(barrier, len(peers))

    def send_stats(g):
        for i, peer in zip(SPOTS, around):
            slot = SPOTS.index(8 - i)
            push(STAT + g, stats.at[g], st_ext.at[g, slot], peer)

    def sides(sem, ext, r, b):
        if b == 0:
            push(sem, ext.at[r, 0], ext.at[r, 2], left)
        else:
            push(sem, ext.at[r, 1], ext.at[r, 3], right)

    pieces = [(c // 2, at(c % 2, 32)) for c in range(4)]
    for c, (b, rows) in enumerate(pieces):
        push(N_NEAR + c, n_ext.at[0, b, rows, :], n_ext.at[far, b, rows, :], mate)
    for b in range(2):
        sides(N_MID, n_ext, 0, b)
    push(A2, a2.at[0], a2.at[1], partner)
    send_stats(GROUPS)
    for b in range(2):
        push(G_NEAR + b, g_ext.at[0, b], g_ext.at[far, b], mate)

    def hand_on(c):
        b, rows = pieces[c]
        piece = n_ext.at[near, b, rows, :]
        arrive(N_NEAR + c, piece)
        push(N_FAR + b, piece, n_ext.at[far, b, rows, :], onward)
        if c % 2 == 1:
            sides(N_CORNER, n_ext, near, b)

    def project(rows, targets, first, last):
        def one(j):
            for t, dst in enumerate((q_ext, k_ext, v_ext)):
                part = pl.ds(pl.multiple_of(D * t + GW * j, GW), GW)
                made = dot(rows, w[:, part]).astype(BF16)
                if t == 0:
                    made = made * SCALE
                for i, to in enumerate(targets):
                    dst[to : to + OWN, at(j, GW)] = made[OWN * i : OWN * (i + 1)]

        steps(first, last, one)

    hand_on(0)
    hand_on(1)
    for load in loads:
        load.wait()
    arrive(N_MID, n_ext.at[0, 2:4])
    own_row = n_ext[0].reshape(2 * OWN, D)
    project(own_row, (0, OWN), 0, 2)
    hand_on(2)
    project(own_row, (0, OWN), 2, GROUPS)
    hand_on(3)
    for b in range(2):
        arrive(N_FAR + b, n_ext.at[far, b])
        sides(N_CORNER, n_ext, far, b)
    project(n_ext[1:3, 0:2].reshape(2 * OWN, D), (2 * OWN, 4 * OWN), 0, GROUPS)
    arrive(N_CORNER, n_ext.at[1:3, 2:4])
    project(n_ext[1:3, 2:4].reshape(2 * OWN, D), (3 * OWN, 5 * OWN), 0, GROUPS)
    for b in range(2):
        arrive(G_NEAR + b, g_ext.at[near, b])
        push(G_FAR + b, g_ext.at[near, b], g_ext.at[far, b], onward)
        sides(G_MID, g_ext, 0, b)
        sides(G_CORNER, g_ext, near, b)

    place = lax.broadcasted_iota(jnp.int32, (1, EXT), 1) // INSIDE

    def attend(g):
        cols = at(g, GW)
        k4, v4 = k_ext[:, cols], v_ext[:, cols]
        s_buf[...] = dot_t(spread_heads(q_ext[MINE, cols]), k4)
        dp_buf[...] = dot_t(spread_heads(g_ext[0, 0:2, :, cols].reshape(OWN, GW)), v4)
        bias = []
        for b in range(2):
            allowed = jnp.zeros((1, EXT), jnp.int32)
            for r in range(3):
                for p in range(4):
                    c = COLUMN_OF[p] - b
                    if c < 0 or c > 2:
                        continue
                    m = 3 * ROW_OF[r] + c
                    value = 1 if m == 4 else mask_ref[b, m if m < 4 else m - 1]
                    allowed = jnp.where(place == 4 * r + p, value, allowed)
            bias.append(jnp.where(allowed > 0, 0.0, NEG_BIG))
        lane = lax.broadcasted_iota(jnp.int32, (INSIDE, OWN), 1)
        stat = [jnp.zeros((INSIDE, OWN), F32)] * 2
        for h in range(GROUP):
            for b in range(2):
                part = slice(OWN * h + INSIDE * b, OWN * h + INSIDE * (b + 1))
                s = s_buf[part, :] + bias[b]
                top = jnp.max(s, axis=1, keepdims=True)
                e = jnp.exp(s - top)
                total = jnp.sum(e, axis=1, keepdims=True)
                p = e * (1.0 / total)
                w_buf[part, :] = p.astype(BF16)
                dp = dp_buf[part, :]
                inner = jnp.sum(p * dp, axis=1, keepdims=True)
                ds_buf[part, :] = (p * (dp - inner)).astype(BF16)
                stat[b] = jnp.where(lane == h, top + jnp.log(total), stat[b])
                stat[b] = jnp.where(lane == GROUP + h, inner, stat[b])
        stats[g] = jnp.transpose(jnp.concatenate(stat, axis=0))[0:8]
        send_stats(g)
        mixed = pick_heads(dot(w_buf[...], v4)).astype(BF16).astype(F32)
        dq_all[:, cols] = (pick_heads(dot(ds_buf[...], k4)) * SCALE).astype(BF16)
        out_v[:, :, cols] = (fields_ref[:, :, cols].astype(F32) + tile_of(mixed)).astype(BF16)

    def offer(u, first, second):
        for half in range(2):
            part = slice(HW * half, HW * (half + 1))
            b_own[u, half] = jnp.concatenate([first[:, part], second[:, part]], axis=1)
        push(PAIR + u, b_own.at[u, 1 - core], b_other.at[u], partner)

    def weigh(u):
        arrive(PAIR + u, b_other.at[u])
        both = jnp.concatenate([b_own[u, core], b_other[u]], axis=0)
        for part in range(4):
            rows = slice(256 * part, 256 * (part + 1))
            left_side = jnp.concatenate([a2[0, rows, :], a2[1, rows, :]], axis=1)
            w_send[u, part] = dot(left_side, both).astype(BF16).reshape(4, 2, 32, UW)
        for slot, d in enumerate(SIBLINGS):
            push(ONE + u, w_send.at[u, x_at[d], :, 0], r1.at[u, 0, slot], x_peer[d])
            push(ONE + u, w_send.at[u, :, y_at[d], 1], r1.at[u, 1, slot], y_peer[d])

    def sum_one(u):
        arrive(ONE + u, r1.at[u])
        for i in range(4):
            acc = w_send[u, x, i, 0].astype(F32)
            for slot in range(3):
                acc = acc + r1[u, 0, slot, i].astype(F32)
            s1[u, 0, i] = acc.astype(BF16)
            acc = w_send[u, i, yi, 1].astype(F32)
            for slot in range(3):
                acc = acc + r1[u, 1, slot, i].astype(F32)
            s1[u, 1, i] = acc.astype(BF16)
        for slot, d in enumerate(SIBLINGS):
            push(TWO + u, s1.at[u, 0, y_at[d]], r2.at[u, 0, slot], y_peer[d])
            push(TWO + u, s1.at[u, 1, x_at[d]], r2.at[u, 1, slot], x_peer[d])

    def sum_two(batch):
        for j in range(3):
            u = 3 * batch + j
            arrive(TWO + u, r2.at[u])
            for colour, mine in ((0, yi), (1, x)):
                acc = s1[u, colour, mine].astype(F32)
                for slot in range(3):
                    acc = acc + r2[u, colour, slot].astype(F32)
                for zz in range(4):
                    made = acc[8 * zz : 8 * zz + 8].astype(BF16)
                    s2[batch, 4 * colour + zz, :, UW * j : UW * (j + 1)] = made
        for slot, d in enumerate(FAR_FIRST):
            push(THREE + batch, s2.at[batch, z_at[d]], r3.at[batch, slot], z_peer[d])

    steps(0, 2, attend)
    offer(0, dq_all[:, 0:GW], dq_all[:, GW : 2 * GW])
    for b in range(2):
        arrive(G_FAR + b, g_ext.at[far, b])
        sides(G_CORNER, g_ext, far, b)
    attend(2)
    arrive(A2, a2.at[1])
    weigh(0)
    attend(3)
    offer(1, dq_all[:, 2 * GW : 3 * GW], dq_all[:, 3 * GW :])
    store_out = pltpu.make_async_copy(out_v, out_hbm, local_sem.at[0])
    store_out.start()

    arrive(G_MID, g_ext.at[0, 2:4])
    arrive(G_CORNER, g_ext.at[1:3, 2:4])
    arrive(STAT + GROUPS, st_ext.at[GROUPS])

    def lanes_of(g):
        low = lax.broadcasted_iota(jnp.int32, (8, OWN), 1) < INSIDE

        def spot(i):
            return st_ext[g, SPOTS.index(i)]

        parts = []
        for r in range(3):
            first = 3 * ROW_OF[r]
            parts.append(stats[g] if r == 0 else spot(first + 1))
            parts.append(jnp.where(low, spot(first + 2), spot(first)))
        return jnp.concatenate(parts, axis=1)

    def keys(g):
        cols = at(g, GW)
        arrive(STAT + g, st_ext.at[g])
        q4 = q_ext[:, cols]
        g4 = g_ext[:, :, :, cols].reshape(EXT, GW)
        s_buf[...] = dot_t(spread_heads(k_ext[MINE, cols]), q4)
        dp_buf[...] = dot_t(spread_heads(v_ext[MINE, cols]), g4)
        stat, brick_masks = lanes_of(g), lanes_of(GROUPS)
        bias = []
        for b in range(2):
            allowed = jnp.zeros((1, EXT), F32)
            for r in range(3):
                for p in range(4):
                    c = b + 2 - COLUMN_OF[p]
                    if c < 0 or c > 2:
                        continue
                    m = 3 * (2 - ROW_OF[r]) + c
                    j = m if m < 4 else m - 1
                    value = jnp.ones((1, EXT), F32) if m == 4 else brick_masks[j : j + 1, :]
                    allowed = jnp.where(place == 4 * r + p, value, allowed)
            bias.append(jnp.where(allowed > 0.5, 0.0, NEG_BIG))
        for h in range(GROUP):
            inner = stat[GROUP + h : GROUP + h + 1, :]
            for b in range(2):
                part = slice(OWN * h + INSIDE * b, OWN * h + INSIDE * (b + 1))
                p = jnp.exp(s_buf[part, :] + (bias[b] - stat[h : h + 1, :]))
                w_buf[part, :] = p.astype(BF16)
                ds_buf[part, :] = (p * (dp_buf[part, :] - inner)).astype(BF16)
        dv4 = pick_heads(dot(w_buf[...], g4)).astype(BF16)
        dk4 = pick_heads(dot(ds_buf[...], q4)).astype(BF16)
        dk_all[:, cols] = dk4
        dv_all[:, cols] = dv4
        offer(g + 2, dk4, dv4)
        weigh(g + 1)

        @pl.when(g > 0)
        def _():
            sum_one(g - 1)

    steps(0, GROUPS, keys)
    weigh(GROUPS + 1)

    grads = (dq_all[...], dk_all[...], dv_all[...])
    parts = []
    for j in range(4):
        rows = at(j, GW)
        made = dot_t(grads[0], w[rows, 0:D])
        made = made + dot_t(grads[1], w[rows, D : 2 * D])
        parts.append(made + dot_t(grads[2], w[rows, 2 * D : 3 * D]))
    gn = jnp.concatenate(parts, axis=1)
    xf = bricks_of(fields_ref[...].astype(F32))
    inv = lax.rsqrt(jnp.mean(xf * xf, axis=1, keepdims=True) + EPSILON)
    total = jnp.sum(gn * xf * inv, axis=0, keepdims=True)
    for i in range(8):
        h0[i : i + 1, :] = total[:, 128 * i : 128 * (i + 1)]
    for slot, d in enumerate(SIBLINGS):
        push(GAIN, h0, h1.at[slot], x_peer[d])
    sum_one(3)
    s = gn * gain_ref[...]
    back = inv * (s - xf * inv * inv * jnp.mean(s * xf, axis=1, keepdims=True))
    gin_v[...] = (grad_ref[...].astype(F32) + tile_of(back)).astype(BF16)
    store_gin = pltpu.make_async_copy(gin_v, gin_hbm, local_sem.at[1])
    store_gin.start()

    sum_one(4)
    sum_two(0)
    arrive(GAIN, h1)
    t1[...] = h0[...] + h1[0] + h1[1] + h1[2]
    for slot, d in enumerate(SIBLINGS):
        push(GAIN + 1, t1, h2.at[slot], y_peer[d])
    sum_one(5)
    arrive(GAIN + 1, h2)
    t2[...] = t1[...] + h2[0] + h2[1] + h2[2]
    for slot, d in enumerate(FAR_FIRST):
        push(GAIN + 2, t2, h3.at[slot], z_peer[d])
    sum_two(1)

    arrive(GAIN + 2, h3)
    tot = t2[...]
    for slot in range(7):
        tot = tot + h3[slot]
    t3[...] = tot
    push(GAIN + 3, t3, h4, partner)
    for batch in range(2):
        arrive(THREE + batch, r3.at[batch])
        acc = s2[batch, z].astype(F32)
        for slot in range(7):
            acc = acc + r3[batch, slot].astype(F32)
        acc = acc * (ALL_TOKENS ** (-0.5))
        fin[0, batch] = acc[0:4]
        fin[1, batch] = acc[4:8]
    push(FOUR, fin.at[1 - core], r4, partner)

    for c, (b, rows) in enumerate(pieces):
        leave(N_NEAR + c, n_ext.at[0, b, rows, :])
    for b in range(2):
        leave(N_FAR + b, n_ext.at[0, b])
        leave(G_NEAR + b, g_ext.at[0, b])
        leave(G_FAR + b, g_ext.at[0, b])
    for sem, ext in ((N_MID, n_ext), (G_MID, g_ext)):
        leave(sem, ext.at[0, 2:4])
        leave(sem + 1, ext.at[1:3, 2:4])
    leave(A2, a2.at[0])
    for g in range(GROUPS + 1):
        leave(STAT + g, st_ext.at[g])
    for u in range(UNITS):
        leave(PAIR + u, b_other.at[u])
        leave(ONE + u, r1.at[u])
        leave(TWO + u, r2.at[u])
    for batch in range(2):
        leave(THREE + batch, r3.at[batch])
    for i, ref in enumerate((h1, h2, h3, h4)):
        leave(GAIN + i, ref)
    store_out.wait()
    store_gin.wait()

    arrive(GAIN + 3, h4)
    summed = (t3[...] + h4[...]) * (ALL_TOKENS ** (-0.5))
    t1[...] = summed
    gg_ref[...] = pltpu.roll(t1[pl.ds(gx, 1), :], lax.rem(128 - 4 * gy, 128), 1)
    arrive(FOUR, r4)
    leave(FOUR, r4)
    for batch in range(2):
        mine, other = fin[core, batch], r4[batch]
        is_first = jnp.broadcast_to(core, mine.shape) == 0
        halves = (jnp.where(is_first, mine, other), jnp.where(is_first, other, mine))
        for j in range(3):
            u = 3 * batch + j
            for i in range(2):
                base = GW * (2 * u + i) if u < 2 else D * (1 + i) + GW * (u - 2)
                come = UW * j + HW * i
                for half in range(2):
                    to = base + HW * half
                    wg_ref[:, to : to + HW] = halves[half][:, come : come + HW]


def layer_call(mask, fields, grad_out, gain, w):
    dma = pltpu.SemaphoreType.DMA
    vm = pltpu.VMEM
    tile = (8, 128)
    stack = (GROUP * OWN, EXT)
    return pl.pallas_call(
        layer_kernel,
        out_shape=(
            jax.ShapeDtypeStruct(fields.shape, BF16),
            jax.ShapeDtypeStruct(fields.shape, BF16),
            jax.ShapeDtypeStruct((4, 3 * D), F32),
            jax.ShapeDtypeStruct((1, 128), F32),
        ),
        in_specs=[SM, VM, VM, VM, ANY],
        out_specs=(ANY, ANY, VM, VM),
        scratch_shapes=[
            vm((D, 3 * D), BF16),
            vm((3, 4, INSIDE, D), BF16), vm((3, 4, INSIDE, D), BF16),
            vm((2, D, OWN), BF16),
            vm((EXT, D), BF16), vm((EXT, D), BF16), vm((EXT, D), BF16),
            vm((OWN, D), BF16), vm((OWN, D), BF16), vm((OWN, D), BF16),
            vm(stack, F32), vm(stack, F32), vm(stack, BF16), vm(stack, BF16),
            vm((GROUPS + 1,) + tile, F32), vm((GROUPS + 1, 8) + tile, F32),
            vm(fields.shape, BF16), vm(fields.shape, BF16),
            vm((UNITS, 2, OWN, UW), BF16), vm((UNITS, OWN, UW), BF16),
            vm((UNITS, 4, 4, 2, 32, UW), BF16),
            vm((UNITS, 2, 3, 4, 32, UW), BF16),
            vm((UNITS, 2, 4, 32, UW), BF16),
            vm((UNITS, 2, 3, 32, UW), BF16),
            vm((2, 8, 8, 3 * UW), BF16),
            vm((2, 7, 8, 3 * UW), BF16),
            vm((2, 2, 4, 3 * UW), F32),
            vm((2, 4, 3 * UW), F32),
            vm(tile, F32), vm((3,) + tile, F32),
            vm(tile, F32), vm((3,) + tile, F32),
            vm(tile, F32), vm((7,) + tile, F32),
            vm(tile, F32), vm(tile, F32),
            dma((3,)), dma((SEMS,)), dma((SEMS,)),
        ],
        compiler_params=pltpu.CompilerParams(
            collective_id=0, has_side_effects=True, vmem_limit_bytes=VMEM_LIMIT
        ),
        name="layer",
    )(mask, fields, grad_out, gain, w)


def finish_kernel(out_in, gin_in, wg_in, gg_in, out, gin, wg, gg):
    out[...] = out_in[...]
    gin[...] = gin_in[...]
    wg[...] = wg_in[...]
    for i in range(4):
        gg[i] = gg_in[0, i]


def finish_call(output, grad_in, w_grad, gains):
    return pl.pallas_call(
        finish_kernel,
        out_shape=(
            jax.ShapeDtypeStruct(output.shape, BF16),
            jax.ShapeDtypeStruct(grad_in.shape, BF16),
            jax.ShapeDtypeStruct(w_grad.shape, F32),
            jax.ShapeDtypeStruct((4,), F32),
        ),
        in_specs=[VM] * 4,
        out_specs=(VM, VM, VM, SM),
        name="finish",
    )(output, grad_in, w_grad, gains)


def per_device(fields, grad_out, norm_gain, w_qkv, brick_mask):
    made = layer_call(
        brick_mask.reshape(2, 8), fields, grad_out, norm_gain.reshape(1, D), w_qkv
    )
    return finish_call(*made)


def solution(mesh):
    placed = (P("gx", "gy", None), P("gx", "gy", None), P(), P(), P("gx", "gy", None))
    return jax.shard_map(
        per_device,
        mesh=mesh,
        in_specs=placed,
        out_specs=(
            P("gx", "gy", None),
            P("gx", "gy", None),
            P(("gx", "gy"), None),
            P(("gx", "gy")),
        ),
        check_vma=False,
    )
```

```python
import jax
import jax.numpy as jnp
from jax import lax
from jax.experimental import pallas as pl
from jax.experimental.pallas import tpu as pltpu
from jax.sharding import PartitionSpec as P

HEADS = 16
BRICK = 8
D = 1024
HD = 64
GROUP = 4
GW = GROUP * HD
INSIDE = BRICK * BRICK
OWN = 2 * INSIDE
EXT = 12 * INSIDE
EPSILON = 1e-05
NEG_BIG = -1e30
SCALE = HD ** (-0.5)
ALL_TOKENS = 32768
MESH = pl.DeviceIdType.MESH
F32 = jnp.float32
BF16 = jnp.bfloat16
ANY = pl.BlockSpec(memory_space=pl.ANY)
VM = pl.BlockSpec(memory_space=pltpu.VMEM)
SM = pl.BlockSpec(memory_space=pltpu.SMEM)
VMEM_LIMIT = 56 * 1024 * 1024

ROW_OF = (1, 0, 2)
COLUMN_OF = (1, 2, 3, 0)


def brick_of(tile, b):
    part = tile[:, BRICK * b : BRICK * (b + 1), :]
    return part.reshape(INSIDE, part.shape[-1])


def tile_of(bricks):
    width = bricks.shape[-1]
    first = bricks[:INSIDE].reshape(BRICK, BRICK, width)
    second = bricks[INSIDE:].reshape(BRICK, BRICK, width)
    return jnp.concatenate([first, second], axis=1)


def shifted(gx, gy, dx, dy):
    nx, ny = lax.axis_size("gx"), lax.axis_size("gy")
    return {"gx": lax.rem(gx + dx + nx, nx), "gy": lax.rem(gy + dy + ny, ny)}


def dot(a, b):
    return lax.dot_general(a, b, (((1,), (0,)), ((), ())), preferred_element_type=F32)


def dot_t(a, b):
    return lax.dot_general(a, b, (((1,), (1,)), ((), ())), preferred_element_type=F32)


def head_lanes(shape):
    return lax.broadcasted_iota(jnp.int32, shape, 1) // HD


def spread_heads(block):
    lanes = head_lanes(block.shape)
    zero = jnp.zeros_like(block)
    return jnp.concatenate([jnp.where(lanes == h, block, zero) for h in range(GROUP)], axis=0)


def pick_heads(stacked):
    lanes = head_lanes((OWN, GW))
    out = stacked[:OWN]
    for h in range(1, GROUP):
        out = jnp.where(lanes == h, stacked[OWN * h : OWN * (h + 1)], out)
    return out


def bricks_of(tile):
    return jnp.concatenate([brick_of(tile, 0), brick_of(tile, 1)], axis=0)


def at(index, size):
    start = index * size
    return pl.ds(start if isinstance(start, int) else pl.multiple_of(start, size), size)


def steps(first, last, body):
    def once(g, carry):
        body(g)
        return carry

    lax.fori_loop(first, last, once, 0)


GROUPS = HEADS // GROUP
HW = GW // 2
UNITS = 6
UW = 2 * HW
BATCHES = ((1, 2, 3), (4, 5))
SPOTS = (0, 1, 2, 3, 5, 6, 7, 8)
MINE = slice(0, OWN)
SIBLINGS = (2, 1, 3)
FAR_FIRST = (4, 3, 5, 2, 6, 1, 7)
(N_NEAR, N_FAR, N_MID, N_CORNER, G_NEAR, G_FAR, G_MID, G_CORNER, A2, STAT, PAIR, ONE, TWO, THREE,
 FOUR, GAIN, SEMS) = (0, 4, 6, 7, 8, 10, 12, 13, 14, 15, 20, 26, 32, 38, 41, 42, 46)


def layer_kernel(
    mask_ref, fields_hbm, grad_hbm, gain_ref, w_hbm,
    out_hbm, gin_hbm, wg_ref, gg_ref,
    fields_ref, grad_ref, w, n_ext, g_ext, a2, q_ext, k_ext, v_ext, dq_all, dk_all, dv_all,
    s_buf, dp_buf, w_buf, ds_buf, stats, st_ext, out_v, gin_v,
    b_own, b_other, w_send, r1, s1, r2, s2, r3, fin, r4,
    z_send, z_r1, z_s1, z_r2, z_s2, z_r3,
    h0, h1, t1, h2, t2, h3, t3, h4,
    local_sem, send, recv,
):
    gx, gy = lax.axis_index("gx"), lax.axis_index("gy")
    left, right = shifted(gx, gy, 0, -1), shifted(gx, gy, 0, 1)
    around = [shifted(gx, gy, i // 3 - 1, i % 3 - 1) for i in SPOTS]
    odd = lax.rem(gx, 2)
    x, yi = gx // 2, 2 * odd + gy // 16
    z, core = lax.rem(gy, 16) // 2, lax.rem(gy, 2)

    def device(x_, yi_, z_, core_):
        return {"gx": 2 * x_ + yi_ // 2, "gy": 16 * lax.rem(yi_, 2) + 2 * z_ + core_}

    partner = device(x, yi, z, 1 - core)
    x_at = [lax.rem(x + d, 4) for d in range(4)]
    y_at = [lax.rem(yi + d, 4) for d in range(4)]
    z_at = [lax.rem(z + d, 8) for d in range(8)]
    x_peer = [device(x_at[d], yi, z, core) for d in range(4)]
    y_peer = [device(x, y_at[d], z, core) for d in range(4)]
    z_peer = [device(x, yi, z_at[d], core) for d in range(8)]
    mate = {"gx": gx + 1 - 2 * odd, "gy": gy}
    onward = {"gx": lax.rem(gx + 2 + 4 * odd, 8), "gy": gy}
    near, far = 2 - odd, 1 + odd

    def copy_of(i, src, dst, peer):
        return pltpu.make_async_remote_copy(
            src_ref=src, dst_ref=dst, send_sem=send.at[i], recv_sem=recv.at[i],
            device_id=peer, device_id_type=MESH,
        )

    def push(i, src, dst, peer):
        copy_of(i, src, dst, peer).start()

    def arrive(i, ref):
        copy_of(i, ref, ref, partner).wait_recv()

    def leave(i, ref):
        copy_of(i, ref, ref, partner).wait_send()

    tiles = [
        pltpu.make_async_copy(fields_hbm, fields_ref, local_sem.at[3]),
        pltpu.make_async_copy(grad_hbm, grad_ref, local_sem.at[4]),
    ]
    for load in tiles:
        load.start()
    loads = [
        pltpu.make_async_copy(w_hbm.at[:, at(t, D)], w.at[:, at(t, D)], local_sem.at[t])
        for t in range(3)
    ]
    for load in loads:
        load.start()

    peers = around + x_peer[1:] + y_peer[1:] + z_peer[1:]
    barrier = pltpu.get_barrier_semaphore()
    for peer in peers:
        pl.semaphore_signal(barrier, inc=1, device_id=peer, device_id_type=MESH)

    for load in tiles:
        load.wait()
    xf = bricks_of(fields_ref[...].astype(F32))
    inv = lax.rsqrt(jnp.mean(xf * xf, axis=1, keepdims=True) + EPSILON)
    n = (xf * inv * gain_ref[...]).astype(BF16)
    n_ext[0, 0:2] = n.reshape(2, INSIDE, D)
    a2[0] = jnp.transpose(n.astype(F32)).astype(BF16)
    g_ext[0, 0:2] = bricks_of(grad_ref[...].astype(F32)).astype(BF16).reshape(2, INSIDE, D)
    lane = lax.broadcasted_iota(jnp.int32, (1, OWN), 1)
    for j in range(8):
        row = jnp.where(lane < INSIDE, mask_ref[0, j], mask_ref[1, j])
        stats[GROUPS, j : j + 1, :] = row.astype(F32)
    pl.semaphore_wait(barrier, len(peers))

    def send_stats(g):
        for i, peer in zip(SPOTS, around):
            slot = SPOTS.index(8 - i)
            push(STAT + g, stats.at[g], st_ext.at[g, slot], peer)

    def sides(sem, ext, r, b):
        if b == 0:
            push(sem, ext.at[r, 0], ext.at[r, 2], left)
        else:
            push(sem, ext.at[r, 1], ext.at[r, 3], right)

    pieces = [(c // 2, at(c % 2, 32)) for c in range(4)]
    for c, (b, rows) in enumerate(pieces):
        push(N_NEAR + c, n_ext.at[0, b, rows, :], n_ext.at[far, b, rows, :], mate)
    for b in range(2):
        sides(N_MID, n_ext, 0, b)
    push(A2, a2.at[0], a2.at[1], partner)
    send_stats(GROUPS)

    def hand_on(c):
        b, rows = pieces[c]
        piece = n_ext.at[near, b, rows, :]
        arrive(N_NEAR + c, piece)
        push(N_FAR + b, piece, n_ext.at[far, b, rows, :], onward)
        if c % 2 == 1:
            sides(N_CORNER, n_ext, near, b)

    def hand_grad_on(b):
        arrive(G_NEAR + b, g_ext.at[near, b])
        push(G_FAR + b, g_ext.at[near, b], g_ext.at[far, b], onward)
        sides(G_CORNER, g_ext, near, b)

    def project(rows, targets, first, last):
        def one(j):
            for t, dst in enumerate((q_ext, k_ext, v_ext)):
                part = pl.ds(pl.multiple_of(D * t + GW * j, GW), GW)
                made = dot(rows, w[:, part]).astype(BF16)
                if t == 0:
                    made = made * SCALE
                for i, to in enumerate(targets):
                    dst[to : to + OWN, at(j, GW)] = made[OWN * i : OWN * (i + 1)]

        steps(first, last, one)

    hand_on(0)
    hand_on(1)
    for load in loads:
        load.wait()
    arrive(N_MID, n_ext.at[0, 2:4])
    own_row = n_ext[0].reshape(2 * OWN, D)
    project(own_row, (0, OWN), 0, 2)
    hand_on(2)
    project(own_row, (0, OWN), 2, GROUPS)
    hand_on(3)
    for b in range(2):
        push(G_NEAR + b, g_ext.at[0, b], g_ext.at[far, b], mate)
    for b in range(2):
        arrive(N_FAR + b, n_ext.at[far, b])
        sides(N_CORNER, n_ext, far, b)
    for b in range(2):
        sides(G_MID, g_ext, 0, b)
    project(n_ext[1:3, 0:2].reshape(2 * OWN, D), (2 * OWN, 4 * OWN), 0, GROUPS)
    hand_grad_on(0)
    arrive(N_CORNER, n_ext.at[1:3, 2:4])
    project(n_ext[1:3, 2:4].reshape(2 * OWN, D), (3 * OWN, 5 * OWN), 0, GROUPS)
    hand_grad_on(1)

    place = lax.broadcasted_iota(jnp.int32, (1, EXT), 1) // INSIDE

    def attend(g):
        cols = at(g, GW)
        k4, v4 = k_ext[:, cols], v_ext[:, cols]
        s_buf[...] = dot_t(spread_heads(q_ext[MINE, cols]), k4)
        dp_buf[...] = dot_t(spread_heads(g_ext[0, 0:2, :, cols].reshape(OWN, GW)), v4)
        bias = []
        for b in range(2):
            allowed = jnp.zeros((1, EXT), jnp.int32)
            for r in range(3):
                for p in range(4):
                    c = COLUMN_OF[p] - b
                    if c < 0 or c > 2:
                        continue
                    m = 3 * ROW_OF[r] + c
                    value = 1 if m == 4 else mask_ref[b, m if m < 4 else m - 1]
                    allowed = jnp.where(place == 4 * r + p, value, allowed)
            bias.append(jnp.where(allowed > 0, 0.0, NEG_BIG))
        lane = lax.broadcasted_iota(jnp.int32, (INSIDE, OWN), 1)
        stat = [jnp.zeros((INSIDE, OWN), F32)] * 2
        for h in range(GROUP):
            for b in range(2):
                part = slice(OWN * h + INSIDE * b, OWN * h + INSIDE * (b + 1))
                s = s_buf[part, :] + bias[b]
                top = jnp.max(s, axis=1, keepdims=True)
                e = jnp.exp(s - top)
                total = jnp.sum(e, axis=1, keepdims=True)
                p = e * (1.0 / total)
                w_buf[part, :] = p.astype(BF16)
                dp = dp_buf[part, :]
                inner = jnp.sum(p * dp, axis=1, keepdims=True)
                ds_buf[part, :] = (p * (dp - inner)).astype(BF16)
                stat[b] = jnp.where(lane == h, top + jnp.log(total), stat[b])
                stat[b] = jnp.where(lane == GROUP + h, inner, stat[b])
        stats[g] = jnp.transpose(jnp.concatenate(stat, axis=0))[0:8]
        send_stats(g)
        mixed = pick_heads(dot(w_buf[...], v4)).astype(BF16).astype(F32)
        dq_all[:, cols] = (pick_heads(dot(ds_buf[...], k4)) * SCALE).astype(BF16)
        out_v[:, :, cols] = (fields_ref[:, :, cols].astype(F32) + tile_of(mixed)).astype(BF16)

    def offer(u, first, second):
        for half in range(2):
            part = slice(HW * half, HW * (half + 1))
            b_own[u, half] = jnp.concatenate([first[:, part], second[:, part]], axis=1)
        push(PAIR + u, b_own.at[u, 1 - core], b_other.at[u], partner)

    def weigh(u):
        arrive(PAIR + u, b_other.at[u])
        both = jnp.concatenate([b_own[u, core], b_other[u]], axis=0)
        for part in range(4):
            rows = slice(256 * part, 256 * (part + 1))
            left_side = jnp.concatenate([a2[0, rows, :], a2[1, rows, :]], axis=1)
            w_send[u, part] = dot(left_side, both).astype(BF16).reshape(4, 2, 32, UW)
        for slot, d in enumerate(SIBLINGS):
            push(ONE + u, w_send.at[u, x_at[d], :, 0], r1.at[u, 0, slot], x_peer[d])
            push(ONE + u, w_send.at[u, :, y_at[d], 1], r1.at[u, 1, slot], y_peer[d])

    def weigh_z():
        arrive(PAIR, b_other.at[0])
        both = jnp.concatenate([b_own[0, core], b_other[0]], axis=0)
        for part in range(4):
            rows = slice(256 * part, 256 * (part + 1))
            left_side = jnp.concatenate([a2[0, rows, :], a2[1, rows, :]], axis=1)
            made = dot(left_side, both)
            for i in range(32):
                z_send[i % 8, part, i // 8] = made[8 * i : 8 * i + 8].astype(BF16)
        for slot, d in enumerate(FAR_FIRST):
            push(ONE, z_send.at[z_at[d]], z_r1.at[slot], z_peer[d])

    def sum_z_one():
        arrive(ONE, z_r1)
        for i in range(4):
            acc = z_send[z, i].astype(F32)
            for slot in range(7):
                acc = acc + z_r1[slot, i].astype(F32)
            z_s1[i] = acc.astype(BF16)
        for slot, d in enumerate(SIBLINGS):
            push(TWO, z_s1.at[x_at[d]], z_r2.at[slot], x_peer[d])

    def sum_z_two():
        arrive(TWO, z_r2)
        acc = z_s1[x].astype(F32)
        for slot in range(3):
            acc = acc + z_r2[slot].astype(F32)
        z_s2[...] = acc.astype(BF16)
        for slot, d in enumerate(SIBLINGS):
            push(THREE + 2, z_s2.at[y_at[d]], z_r3.at[slot], y_peer[d])

    def sum_one(u):
        arrive(ONE + u, r1.at[u])
        for i in range(4):
            acc = w_send[u, x, i, 0].astype(F32)
            for slot in range(3):
                acc = acc + r1[u, 0, slot, i].astype(F32)
            s1[u, 0, i] = acc.astype(BF16)
            acc = w_send[u, i, yi, 1].astype(F32)
            for slot in range(3):
                acc = acc + r1[u, 1, slot, i].astype(F32)
            s1[u, 1, i] = acc.astype(BF16)
        for slot, d in enumerate(SIBLINGS):
            push(TWO + u, s1.at[u, 0, y_at[d]], r2.at[u, 0, slot], y_peer[d])
            push(TWO + u, s1.at[u, 1, x_at[d]], r2.at[u, 1, slot], x_peer[d])

    def sum_two(batch):
        for j, u in enumerate(BATCHES[batch]):
            arrive(TWO + u, r2.at[u])
            for colour, mine in ((0, yi), (1, x)):
                acc = s1[u, colour, mine].astype(F32)
                for slot in range(3):
                    acc = acc + r2[u, colour, slot].astype(F32)
                for zz in range(4):
                    made = acc[8 * zz : 8 * zz + 8].astype(BF16)
                    s2[batch, 4 * colour + zz, :, UW * j : UW * (j + 1)] = made
        wide = slice(0, UW * len(BATCHES[batch]))
        for slot, d in enumerate(FAR_FIRST):
            push(
                THREE + batch, s2.at[batch, z_at[d], :, wide], r3.at[batch, slot, :, wide], z_peer[d]
            )

    steps(0, 2, attend)
    offer(0, dq_all[:, 0:GW], dq_all[:, GW : 2 * GW])
    attend(2)
    arrive(A2, a2.at[1])
    weigh_z()
    for b in range(2):
        arrive(G_FAR + b, g_ext.at[far, b])
        sides(G_CORNER, g_ext, far, b)
    attend(3)
    offer(1, dq_all[:, 2 * GW : 3 * GW], dq_all[:, 3 * GW :])
    store_out = pltpu.make_async_copy(out_v, out_hbm, local_sem.at[0])
    store_out.start()

    arrive(G_MID, g_ext.at[0, 2:4])
    arrive(G_CORNER, g_ext.at[1:3, 2:4])
    arrive(STAT + GROUPS, st_ext.at[GROUPS])

    def lanes_of(g):
        low = lax.broadcasted_iota(jnp.int32, (8, OWN), 1) < INSIDE

        def spot(i):
            return st_ext[g, SPOTS.index(i)]

        parts = []
        for r in range(3):
            first = 3 * ROW_OF[r]
            parts.append(stats[g] if r == 0 else spot(first + 1))
            parts.append(jnp.where(low, spot(first + 2), spot(first)))
        return jnp.concatenate(parts, axis=1)

    def keys(g):
        cols = at(g, GW)
        arrive(STAT + g, st_ext.at[g])
        q4 = q_ext[:, cols]
        g4 = g_ext[:, :, :, cols].reshape(EXT, GW)
        s_buf[...] = dot_t(spread_heads(k_ext[MINE, cols]), q4)
        dp_buf[...] = dot_t(spread_heads(v_ext[MINE, cols]), g4)
        stat, brick_masks = lanes_of(g), lanes_of(GROUPS)
        bias = []
        for b in range(2):
            allowed = jnp.zeros((1, EXT), F32)
            for r in range(3):
                for p in range(4):
                    c = b + 2 - COLUMN_OF[p]
                    if c < 0 or c > 2:
                        continue
                    m = 3 * (2 - ROW_OF[r]) + c
                    j = m if m < 4 else m - 1
                    value = jnp.ones((1, EXT), F32) if m == 4 else brick_masks[j : j + 1, :]
                    allowed = jnp.where(place == 4 * r + p, value, allowed)
            bias.append(jnp.where(allowed > 0.5, 0.0, NEG_BIG))
        for h in range(GROUP):
            inner = stat[GROUP + h : GROUP + h + 1, :]
            for b in range(2):
                part = slice(OWN * h + INSIDE * b, OWN * h + INSIDE * (b + 1))
                p = jnp.exp(s_buf[part, :] + (bias[b] - stat[h : h + 1, :]))
                w_buf[part, :] = p.astype(BF16)
                ds_buf[part, :] = (p * (dp_buf[part, :] - inner)).astype(BF16)
        dv4 = pick_heads(dot(w_buf[...], g4)).astype(BF16)
        dk4 = pick_heads(dot(ds_buf[...], q4)).astype(BF16)
        dk_all[:, cols] = dk4
        dv_all[:, cols] = dv4
        offer(g + 2, dk4, dv4)
        weigh(g + 1)

        @pl.when(g > 1)
        def _():
            sum_one(g - 1)

    steps(0, GROUPS, keys)
    weigh(GROUPS + 1)

    grads = (dq_all[...], dk_all[...], dv_all[...])
    parts = []
    for j in range(4):
        rows = at(j, GW)
        made = dot_t(grads[0], w[rows, 0:D])
        made = made + dot_t(grads[1], w[rows, D : 2 * D])
        parts.append(made + dot_t(grads[2], w[rows, 2 * D : 3 * D]))
    gn = jnp.concatenate(parts, axis=1)
    xf = bricks_of(fields_ref[...].astype(F32))
    inv = lax.rsqrt(jnp.mean(xf * xf, axis=1, keepdims=True) + EPSILON)
    total = jnp.sum(gn * xf * inv, axis=0, keepdims=True)
    for i in range(8):
        h0[i : i + 1, :] = total[:, 128 * i : 128 * (i + 1)]
    for slot, d in enumerate(SIBLINGS):
        push(GAIN, h0, h1.at[slot], x_peer[d])
    sum_one(3)
    s = gn * gain_ref[...]
    back = inv * (s - xf * inv * inv * jnp.mean(s * xf, axis=1, keepdims=True))
    gin_v[...] = (grad_ref[...].astype(F32) + tile_of(back)).astype(BF16)
    store_gin = pltpu.make_async_copy(gin_v, gin_hbm, local_sem.at[1])
    store_gin.start()

    sum_z_one()
    sum_one(4)
    sum_two(0)
    arrive(GAIN, h1)
    t1[...] = h0[...] + h1[0] + h1[1] + h1[2]
    for slot, d in enumerate(SIBLINGS):
        push(GAIN + 1, t1, h2.at[slot], y_peer[d])
    sum_z_two()
    sum_one(5)
    arrive(GAIN + 1, h2)
    t2[...] = t1[...] + h2[0] + h2[1] + h2[2]
    for slot, d in enumerate(FAR_FIRST):
        push(GAIN + 2, t2, h3.at[slot], z_peer[d])
    sum_two(1)

    arrive(GAIN + 2, h3)
    tot = t2[...]
    for slot in range(7):
        tot = tot + h3[slot]
    t3[...] = tot
    push(GAIN + 3, t3, h4, partner)

    def settle(acc, columns):
        acc = acc * (ALL_TOKENS ** (-0.5))
        fin[0, :, columns] = acc[0:4]
        fin[1, :, columns] = acc[4:8]

    arrive(THREE + 2, z_r3)
    acc = z_s2[yi].astype(F32)
    for slot in range(3):
        acc = acc + z_r3[slot].astype(F32)
    settle(acc, slice(0, UW))
    for batch, units in enumerate(BATCHES):
        wide = slice(0, UW * len(units))
        arrive(THREE + batch, r3.at[batch, :, :, wide])
        acc = s2[batch, z, :, wide].astype(F32)
        for slot in range(7):
            acc = acc + r3[batch, slot, :, wide].astype(F32)
        settle(acc, slice(UW * units[0], UW * (units[-1] + 1)))
    push(FOUR, fin.at[1 - core], r4, partner)

    for c, (b, rows) in enumerate(pieces):
        leave(N_NEAR + c, n_ext.at[0, b, rows, :])
    for b in range(2):
        leave(N_FAR + b, n_ext.at[0, b])
        leave(G_NEAR + b, g_ext.at[0, b])
        leave(G_FAR + b, g_ext.at[0, b])
    for sem, ext in ((N_MID, n_ext), (G_MID, g_ext)):
        leave(sem, ext.at[0, 2:4])
        leave(sem + 1, ext.at[1:3, 2:4])
    leave(A2, a2.at[0])
    for g in range(GROUPS + 1):
        leave(STAT + g, st_ext.at[g])
    for u in range(UNITS):
        leave(PAIR + u, b_other.at[u])
        leave(ONE + u, r1.at[u] if u > 0 else z_r1)
        leave(TWO + u, r2.at[u] if u > 0 else z_r2)
    for batch, units in enumerate(BATCHES):
        leave(THREE + batch, r3.at[batch, :, :, 0 : UW * len(units)])
    leave(THREE + 2, z_r3)
    for i, ref in enumerate((h1, h2, h3, h4)):
        leave(GAIN + i, ref)
    store_out.wait()
    store_gin.wait()

    arrive(GAIN + 3, h4)
    summed = (t3[...] + h4[...]) * (ALL_TOKENS ** (-0.5))
    t1[...] = summed
    gg_ref[...] = pltpu.roll(t1[pl.ds(gx, 1), :], lax.rem(128 - 4 * gy, 128), 1)
    arrive(FOUR, r4)
    leave(FOUR, r4)
    mine, other = fin[core], r4[...]
    is_first = jnp.broadcast_to(core, mine.shape) == 0
    halves = (jnp.where(is_first, mine, other), jnp.where(is_first, other, mine))
    for u in range(UNITS):
        for i in range(2):
            base = GW * (2 * u + i) if u < 2 else D * (1 + i) + GW * (u - 2)
            come = UW * u + HW * i
            for half in range(2):
                to = base + HW * half
                wg_ref[:, to : to + HW] = halves[half][:, come : come + HW]


def layer_call(mask, fields, grad_out, gain, w):
    dma = pltpu.SemaphoreType.DMA
    vm = pltpu.VMEM
    tile = (8, 128)
    stack = (GROUP * OWN, EXT)
    return pl.pallas_call(
        layer_kernel,
        out_shape=(
            jax.ShapeDtypeStruct(fields.shape, BF16),
            jax.ShapeDtypeStruct(fields.shape, BF16),
            jax.ShapeDtypeStruct((4, 3 * D), F32),
            jax.ShapeDtypeStruct((1, 128), F32),
        ),
        in_specs=[SM, ANY, ANY, VM, ANY],
        out_specs=(ANY, ANY, VM, VM),
        scratch_shapes=[
            vm(fields.shape, BF16), vm(fields.shape, BF16),
            vm((D, 3 * D), BF16),
            vm((3, 4, INSIDE, D), BF16), vm((3, 4, INSIDE, D), BF16),
            vm((2, D, OWN), BF16),
            vm((EXT, D), BF16), vm((EXT, D), BF16), vm((EXT, D), BF16),
            vm((OWN, D), BF16), vm((OWN, D), BF16), vm((OWN, D), BF16),
            vm(stack, F32), vm(stack, F32), vm(stack, BF16), vm(stack, BF16),
            vm((GROUPS + 1,) + tile, F32), vm((GROUPS + 1, 8) + tile, F32),
            vm(fields.shape, BF16), vm(fields.shape, BF16),
            vm((UNITS, 2, OWN, UW), BF16), vm((UNITS, OWN, UW), BF16),
            vm((UNITS, 4, 4, 2, 32, UW), BF16),
            vm((UNITS, 2, 3, 4, 32, UW), BF16),
            vm((UNITS, 2, 4, 32, UW), BF16),
            vm((UNITS, 2, 3, 32, UW), BF16),
            vm((2, 8, 8, 3 * UW), BF16),
            vm((2, 7, 8, 3 * UW), BF16),
            vm((2, 4, UNITS * UW), F32),
            vm((4, UNITS * UW), F32),
            vm((8, 4, 4, 8, UW), BF16), vm((7, 4, 4, 8, UW), BF16),
            vm((4, 4, 8, UW), BF16), vm((3, 4, 8, UW), BF16),
            vm((4, 8, UW), BF16), vm((3, 8, UW), BF16),
            vm(tile, F32), vm((3,) + tile, F32),
            vm(tile, F32), vm((3,) + tile, F32),
            vm(tile, F32), vm((7,) + tile, F32),
            vm(tile, F32), vm(tile, F32),
            dma((5,)), dma((SEMS,)), dma((SEMS,)),
        ],
        compiler_params=pltpu.CompilerParams(
            collective_id=0, has_side_effects=True, vmem_limit_bytes=VMEM_LIMIT
        ),
        name="layer",
    )(mask, fields, grad_out, gain, w)


def finish_kernel(out_in, gin_in, wg_in, gg_in, out, gin, wg, gg):
    out[...] = out_in[...]
    gin[...] = gin_in[...]
    wg[...] = wg_in[...]
    for i in range(4):
        gg[i] = gg_in[0, i]


def finish_call(output, grad_in, w_grad, gains):
    return pl.pallas_call(
        finish_kernel,
        out_shape=(
            jax.ShapeDtypeStruct(output.shape, BF16),
            jax.ShapeDtypeStruct(grad_in.shape, BF16),
            jax.ShapeDtypeStruct(w_grad.shape, F32),
            jax.ShapeDtypeStruct((4,), F32),
        ),
        in_specs=[VM] * 4,
        out_specs=(VM, VM, VM, SM),
        name="finish",
    )(output, grad_in, w_grad, gains)


def per_device(fields, grad_out, norm_gain, w_qkv, brick_mask):
    made = layer_call(
        brick_mask.reshape(2, 8), fields, grad_out, norm_gain.reshape(1, D), w_qkv
    )
    return finish_call(*made)


def solution(mesh):
    placed = (P("gx", "gy", None), P("gx", "gy", None), P(), P(), P("gx", "gy", None))
    return jax.shard_map(
        per_device,
        mesh=mesh,
        in_specs=placed,
        out_specs=(
            P("gx", "gy", None),
            P("gx", "gy", None),
            P(("gx", "gy"), None),
            P(("gx", "gy")),
        ),
        check_vma=False,
    )
```

```python
import jax
import jax.numpy as jnp
from jax import lax
from jax.experimental import pallas as pl
from jax.experimental.pallas import tpu as pltpu
from jax.sharding import PartitionSpec as P

HEADS = 16
BRICK = 8
D = 1024
HD = 64
GROUP = 4
GW = GROUP * HD
INSIDE = BRICK * BRICK
OWN = 2 * INSIDE
EXT = 12 * INSIDE
EPSILON = 1e-05
NEG_BIG = -1e30
SCALE = HD ** (-0.5)
ALL_TOKENS = 32768
MESH = pl.DeviceIdType.MESH
F32 = jnp.float32
BF16 = jnp.bfloat16
ANY = pl.BlockSpec(memory_space=pl.ANY)
VM = pl.BlockSpec(memory_space=pltpu.VMEM)
SM = pl.BlockSpec(memory_space=pltpu.SMEM)
VMEM_LIMIT = 56 * 1024 * 1024

ROW_OF = (1, 0, 2)
COLUMN_OF = (1, 2, 3, 0)


def brick_of(tile, b):
    part = tile[:, BRICK * b : BRICK * (b + 1), :]
    return part.reshape(INSIDE, part.shape[-1])


def tile_of(bricks):
    width = bricks.shape[-1]
    first = bricks[:INSIDE].reshape(BRICK, BRICK, width)
    second = bricks[INSIDE:].reshape(BRICK, BRICK, width)
    return jnp.concatenate([first, second], axis=1)


def shifted(gx, gy, dx, dy):
    nx, ny = lax.axis_size("gx"), lax.axis_size("gy")
    return {"gx": lax.rem(gx + dx + nx, nx), "gy": lax.rem(gy + dy + ny, ny)}


def dot(a, b):
    return lax.dot_general(a, b, (((1,), (0,)), ((), ())), preferred_element_type=F32)


def dot_t(a, b):
    return lax.dot_general(a, b, (((1,), (1,)), ((), ())), preferred_element_type=F32)


def head_lanes(shape):
    return lax.broadcasted_iota(jnp.int32, shape, 1) // HD


def spread_heads(block):
    lanes = head_lanes(block.shape)
    zero = jnp.zeros_like(block)
    return jnp.concatenate([jnp.where(lanes == h, block, zero) for h in range(GROUP)], axis=0)


def pick_heads(stacked):
    lanes = head_lanes((OWN, GW))
    out = stacked[:OWN]
    for h in range(1, GROUP):
        out = jnp.where(lanes == h, stacked[OWN * h : OWN * (h + 1)], out)
    return out


def bricks_of(tile):
    return jnp.concatenate([brick_of(tile, 0), brick_of(tile, 1)], axis=0)


def at(index, size):
    start = index * size
    return pl.ds(start if isinstance(start, int) else pl.multiple_of(start, size), size)


def steps(first, last, body):
    def once(g, carry):
        body(g)
        return carry

    lax.fori_loop(first, last, once, 0)


GROUPS = HEADS // GROUP
HW = GW // 2
UNITS = 6
UW = 2 * HW
SPOTS = (0, 1, 2, 3, 5, 6, 7, 8)
MINE = slice(0, OWN)
SIBLINGS = (2, 1, 3)
FAR_FIRST = (4, 3, 5, 2, 6, 1, 7)
(N_NEAR, N_FAR, N_MID, N_CORNER, G_NEAR, G_FAR, G_MID, G_CORNER, A2, STAT, PAIR, ONE, TWO, THREE,
 FOUR, GAIN, HALF, SEMS) = (0, 4, 6, 7, 8, 10, 12, 13, 14, 15, 20, 26, 32, 38, 40, 41, 45, 51)


def layer_kernel(
    mask_ref, fields_ref, grad_ref, gain_ref, w_hbm,
    out_hbm, gin_hbm, wg_ref, gg_ref,
    w, n_ext, g_ext, a2, q_ext, k_ext, v_ext, dq_all, dk_all, dv_all,
    s_buf, dp_buf, w_buf, ds_buf, stats, st_ext, out_v, gin_v,
    b_own, b_other, w_send, r1, half, r_half, s1, r2, s2, r3, fin, r4,
    h0, h1, t1, h2, t2, h3, t3, h4,
    local_sem, send, recv,
):
    gx, gy = lax.axis_index("gx"), lax.axis_index("gy")
    left, right = shifted(gx, gy, 0, -1), shifted(gx, gy, 0, 1)
    around = [shifted(gx, gy, i // 3 - 1, i % 3 - 1) for i in SPOTS]
    odd = lax.rem(gx, 2)
    x, yi = gx // 2, 2 * odd + gy // 16
    z, core = lax.rem(gy, 16) // 2, lax.rem(gy, 2)

    def device(x_, yi_, z_, core_):
        return {"gx": 2 * x_ + yi_ // 2, "gy": 16 * lax.rem(yi_, 2) + 2 * z_ + core_}

    partner = device(x, yi, z, 1 - core)
    x_at = [lax.rem(x + d, 4) for d in range(4)]
    y_at = [lax.rem(yi + d, 4) for d in range(4)]
    z_at = [lax.rem(z + d, 8) for d in range(8)]
    x_peer = [device(x_at[d], yi, z, core) for d in range(4)]
    y_peer = [device(x, y_at[d], z, core) for d in range(4)]
    z_peer = [device(x, yi, z_at[d], core) for d in range(8)]
    def trades(c):
        even_pair, odd_pair = c + 1 - 2 * lax.rem(c, 2), 3 - c
        return even_pair + core * (odd_pair - even_pair), odd_pair + core * (even_pair - odd_pair)

    def y_index(p):
        return 2 * lax.rem(p, 2) + p // 2

    fx, sx = trades(x)
    fy, sy = [y_index(p) for p in trades(2 * (gy // 16) + odd)]
    ox, oy = 6 - x - fx - sx, 6 - yi - fy - sy

    mate = {"gx": gx + 1 - 2 * odd, "gy": gy}
    onward = {"gx": lax.rem(gx + 2 + 4 * odd, 8), "gy": gy}
    near, far = 2 - odd, 1 + odd

    def copy_of(i, src, dst, peer):
        return pltpu.make_async_remote_copy(
            src_ref=src, dst_ref=dst, send_sem=send.at[i], recv_sem=recv.at[i],
            device_id=peer, device_id_type=MESH,
        )

    def push(i, src, dst, peer):
        copy_of(i, src, dst, peer).start()

    def arrive(i, ref):
        copy_of(i, ref, ref, partner).wait_recv()

    def leave(i, ref):
        copy_of(i, ref, ref, partner).wait_send()

    loads = [
        pltpu.make_async_copy(w_hbm.at[:, at(t, D)], w.at[:, at(t, D)], local_sem.at[t])
        for t in range(3)
    ]
    for load in loads:
        load.start()

    peers = around + x_peer[1:] + y_peer[1:] + z_peer[1:]
    barrier = pltpu.get_barrier_semaphore()
    for peer in peers:
        pl.semaphore_signal(barrier, inc=1, device_id=peer, device_id_type=MESH)

    xf = bricks_of(fields_ref[...].astype(F32))
    inv = lax.rsqrt(jnp.mean(xf * xf, axis=1, keepdims=True) + EPSILON)
    n = (xf * inv * gain_ref[...]).astype(BF16)
    n_ext[0, 0:2] = n.reshape(2, INSIDE, D)
    a2[0] = jnp.transpose(n.astype(F32)).astype(BF16)
    g_ext[0, 0:2] = bricks_of(grad_ref[...].astype(F32)).astype(BF16).reshape(2, INSIDE, D)
    lane = lax.broadcasted_iota(jnp.int32, (1, OWN), 1)
    for j in range(8):
        row = jnp.where(lane < INSIDE, mask_ref[0, j], mask_ref[1, j])
        stats[GROUPS, j : j + 1, :] = row.astype(F32)
    pl.semaphore_wait(barrier, len(peers))

    def send_stats(g):
        for i, peer in zip(SPOTS, around):
            slot = SPOTS.index(8 - i)
            push(STAT + g, stats.at[g], st_ext.at[g, slot], peer)

    def sides(sem, ext, r, b):
        if b == 0:
            push(sem, ext.at[r, 0], ext.at[r, 2], left)
        else:
            push(sem, ext.at[r, 1], ext.at[r, 3], right)

    pieces = [(c // 2, at(c % 2, 32)) for c in range(4)]
    for c, (b, rows) in enumerate(pieces):
        push(N_NEAR + c, n_ext.at[0, b, rows, :], n_ext.at[far, b, rows, :], mate)
    for b in range(2):
        sides(N_MID, n_ext, 0, b)
    push(A2, a2.at[0], a2.at[1], partner)
    send_stats(GROUPS)

    def hand_on(c):
        b, rows = pieces[c]
        piece = n_ext.at[near, b, rows, :]
        arrive(N_NEAR + c, piece)
        push(N_FAR + b, piece, n_ext.at[far, b, rows, :], onward)
        if c % 2 == 1:
            sides(N_CORNER, n_ext, near, b)

    def hand_grad_on(b):
        arrive(G_NEAR + b, g_ext.at[near, b])
        push(G_FAR + b, g_ext.at[near, b], g_ext.at[far, b], onward)
        sides(G_CORNER, g_ext, near, b)

    def project(rows, targets, first, last):
        def one(j):
            for t, dst in enumerate((q_ext, k_ext, v_ext)):
                part = pl.ds(pl.multiple_of(D * t + GW * j, GW), GW)
                made = dot(rows, w[:, part]).astype(BF16)
                if t == 0:
                    made = made * SCALE
                for i, to in enumerate(targets):
                    dst[to : to + OWN, at(j, GW)] = made[OWN * i : OWN * (i + 1)]

        steps(first, last, one)

    hand_on(0)
    hand_on(1)
    for load in loads:
        load.wait()
    arrive(N_MID, n_ext.at[0, 2:4])
    own_row = n_ext[0].reshape(2 * OWN, D)
    project(own_row, (0, OWN), 0, 2)
    hand_on(2)
    project(own_row, (0, OWN), 2, GROUPS)
    hand_on(3)
    for b in range(2):
        push(G_NEAR + b, g_ext.at[0, b], g_ext.at[far, b], mate)
    for b in range(2):
        arrive(N_FAR + b, n_ext.at[far, b])
        sides(N_CORNER, n_ext, far, b)
    for b in range(2):
        sides(G_MID, g_ext, 0, b)
    project(n_ext[1:3, 0:2].reshape(2 * OWN, D), (2 * OWN, 4 * OWN), 0, GROUPS)
    hand_grad_on(0)
    arrive(N_CORNER, n_ext.at[1:3, 2:4])
    project(n_ext[1:3, 2:4].reshape(2 * OWN, D), (3 * OWN, 5 * OWN), 0, GROUPS)
    hand_grad_on(1)

    place = lax.broadcasted_iota(jnp.int32, (1, EXT), 1) // INSIDE

    def attend(g):
        cols = at(g, GW)
        k4, v4 = k_ext[:, cols], v_ext[:, cols]
        s_buf[...] = dot_t(spread_heads(q_ext[MINE, cols]), k4)
        dp_buf[...] = dot_t(spread_heads(g_ext[0, 0:2, :, cols].reshape(OWN, GW)), v4)
        bias = []
        for b in range(2):
            allowed = jnp.zeros((1, EXT), jnp.int32)
            for r in range(3):
                for p in range(4):
                    c = COLUMN_OF[p] - b
                    if c < 0 or c > 2:
                        continue
                    m = 3 * ROW_OF[r] + c
                    value = 1 if m == 4 else mask_ref[b, m if m < 4 else m - 1]
                    allowed = jnp.where(place == 4 * r + p, value, allowed)
            bias.append(jnp.where(allowed > 0, 0.0, NEG_BIG))
        lane = lax.broadcasted_iota(jnp.int32, (INSIDE, OWN), 1)
        stat = [jnp.zeros((INSIDE, OWN), F32)] * 2
        for h in range(GROUP):
            for b in range(2):
                part = slice(OWN * h + INSIDE * b, OWN * h + INSIDE * (b + 1))
                s = s_buf[part, :] + bias[b]
                top = jnp.max(s, axis=1, keepdims=True)
                e = jnp.exp(s - top)
                total = jnp.sum(e, axis=1, keepdims=True)
                p = e * (1.0 / total)
                w_buf[part, :] = p.astype(BF16)
                dp = dp_buf[part, :]
                inner = jnp.sum(p * dp, axis=1, keepdims=True)
                ds_buf[part, :] = (p * (dp - inner)).astype(BF16)
                stat[b] = jnp.where(lane == h, top + jnp.log(total), stat[b])
                stat[b] = jnp.where(lane == GROUP + h, inner, stat[b])
        stats[g] = jnp.transpose(jnp.concatenate(stat, axis=0))[0:8]
        send_stats(g)
        mixed = pick_heads(dot(w_buf[...], v4)).astype(BF16).astype(F32)
        dq_all[:, cols] = (pick_heads(dot(ds_buf[...], k4)) * SCALE).astype(BF16)
        out_v[:, :, cols] = (fields_ref[:, :, cols].astype(F32) + tile_of(mixed)).astype(BF16)

    def offer(u, first, second):
        for half in range(2):
            part = slice(HW * half, HW * (half + 1))
            b_own[u, half] = jnp.concatenate([first[:, part], second[:, part]], axis=1)
        push(PAIR + u, b_own.at[u, 1 - core], b_other.at[u], partner)

    def weigh(u):
        arrive(PAIR + u, b_other.at[u])
        both = jnp.concatenate([b_own[u, core], b_other[u]], axis=0)
        for part in range(4):
            rows = slice(256 * part, 256 * (part + 1))
            left_side = jnp.concatenate([a2[0, rows, :], a2[1, rows, :]], axis=1)
            w_send[u, part] = dot(left_side, both).astype(BF16).reshape(4, 2, 32, UW)
        for slot, to in enumerate((ox, fx)):
            push(ONE + u, w_send.at[u, to, :, 0], r1.at[u, 0, slot], device(fx, yi, z, core))
        for slot, to in enumerate((oy, fy)):
            push(ONE + u, w_send.at[u, :, to, 1], r1.at[u, 1, slot], device(x, fy, z, core))

    def sum_half(u):
        arrive(ONE + u, r1.at[u])

        def one(i):
            half[u, 0, i] = (w_send[u, sx, i, 0].astype(F32) + r1[u, 0, 0, i].astype(F32)).astype(BF16)
            half[u, 1, i] = (w_send[u, i, sy, 1].astype(F32) + r1[u, 1, 0, i].astype(F32)).astype(BF16)

        steps(0, 4, one)
        push(HALF + u, half.at[u, 0], r_half.at[u, 0], device(sx, yi, z, core))
        push(HALF + u, half.at[u, 1], r_half.at[u, 1], device(x, sy, z, core))

    def sum_one(u):
        arrive(HALF + u, r_half.at[u])

        def one(i):
            acc = w_send[u, x, i, 0].astype(F32) + r1[u, 0, 1, i].astype(F32)
            s1[u, 0, i] = (acc + r_half[u, 0, i].astype(F32)).astype(BF16)
            acc = w_send[u, i, yi, 1].astype(F32) + r1[u, 1, 1, i].astype(F32)
            s1[u, 1, i] = (acc + r_half[u, 1, i].astype(F32)).astype(BF16)

        steps(0, 4, one)
        for slot, d in enumerate(SIBLINGS):
            push(TWO + u, s1.at[u, 0, y_at[d]], r2.at[u, 0, slot], y_peer[d])
            push(TWO + u, s1.at[u, 1, x_at[d]], r2.at[u, 1, slot], x_peer[d])

    def sum_two(batch):
        for j in range(3):
            u = 3 * batch + j
            arrive(TWO + u, r2.at[u])
            for colour, mine in ((0, yi), (1, x)):
                acc = s1[u, colour, mine].astype(F32)
                for slot in range(3):
                    acc = acc + r2[u, colour, slot].astype(F32)
                for zz in range(4):
                    made = acc[8 * zz : 8 * zz + 8].astype(BF16)
                    s2[batch, 4 * colour + zz, :, UW * j : UW * (j + 1)] = made
        for slot, d in enumerate(FAR_FIRST):
            push(THREE + batch, s2.at[batch, z_at[d]], r3.at[batch, slot], z_peer[d])

    def forward(g):
        attend(g)

        @pl.when(g == 1)
        def _():
            offer(0, dq_all[:, 0:GW], dq_all[:, GW : 2 * GW])

        @pl.when(g == 2)
        def _():
            for b in range(2):
                arrive(G_FAR + b, g_ext.at[far, b])
                sides(G_CORNER, g_ext, far, b)
            arrive(A2, a2.at[1])
            weigh(0)

        @pl.when(g == 3)
        def _():
            offer(1, dq_all[:, 2 * GW : 3 * GW], dq_all[:, 3 * GW :])

    steps(0, GROUPS, forward)
    store_out = pltpu.make_async_copy(out_v, out_hbm, local_sem.at[0])
    store_out.start()

    arrive(G_MID, g_ext.at[0, 2:4])
    arrive(G_CORNER, g_ext.at[1:3, 2:4])
    arrive(STAT + GROUPS, st_ext.at[GROUPS])

    def lanes_of(g):
        low = lax.broadcasted_iota(jnp.int32, (8, OWN), 1) < INSIDE

        def spot(i):
            return st_ext[g, SPOTS.index(i)]

        parts = []
        for r in range(3):
            first = 3 * ROW_OF[r]
            parts.append(stats[g] if r == 0 else spot(first + 1))
            parts.append(jnp.where(low, spot(first + 2), spot(first)))
        return jnp.concatenate(parts, axis=1)

    def keys(g):
        cols = at(g, GW)
        arrive(STAT + g, st_ext.at[g])
        q4 = q_ext[:, cols]
        g4 = g_ext[:, :, :, cols].reshape(EXT, GW)
        s_buf[...] = dot_t(spread_heads(k_ext[MINE, cols]), q4)
        dp_buf[...] = dot_t(spread_heads(v_ext[MINE, cols]), g4)
        stat, brick_masks = lanes_of(g), lanes_of(GROUPS)
        bias = []
        for b in range(2):
            allowed = jnp.zeros((1, EXT), F32)
            for r in range(3):
                for p in range(4):
                    c = b + 2 - COLUMN_OF[p]
                    if c < 0 or c > 2:
                        continue
                    m = 3 * (2 - ROW_OF[r]) + c
                    j = m if m < 4 else m - 1
                    value = jnp.ones((1, EXT), F32) if m == 4 else brick_masks[j : j + 1, :]
                    allowed = jnp.where(place == 4 * r + p, value, allowed)
            bias.append(jnp.where(allowed > 0.5, 0.0, NEG_BIG))
        for h in range(GROUP):
            inner = stat[GROUP + h : GROUP + h + 1, :]
            for b in range(2):
                part = slice(OWN * h + INSIDE * b, OWN * h + INSIDE * (b + 1))
                p = jnp.exp(s_buf[part, :] + (bias[b] - stat[h : h + 1, :]))
                w_buf[part, :] = p.astype(BF16)
                ds_buf[part, :] = (p * (dp_buf[part, :] - inner)).astype(BF16)
        dv4 = pick_heads(dot(w_buf[...], g4)).astype(BF16)
        dk4 = pick_heads(dot(ds_buf[...], q4)).astype(BF16)
        dk_all[:, cols] = dk4
        dv_all[:, cols] = dv4
        offer(g + 2, dk4, dv4)
        weigh(g + 1)
        sum_half(g)

        @pl.when(g > 0)
        def _():
            sum_one(g - 1)

    steps(0, GROUPS, keys)
    weigh(GROUPS + 1)

    grads = (dq_all[...], dk_all[...], dv_all[...])
    parts = []
    for j in range(4):
        rows = at(j, GW)
        made = dot_t(grads[0], w[rows, 0:D])
        made = made + dot_t(grads[1], w[rows, D : 2 * D])
        parts.append(made + dot_t(grads[2], w[rows, 2 * D : 3 * D]))
    gn = jnp.concatenate(parts, axis=1)
    xf = bricks_of(fields_ref[...].astype(F32))
    inv = lax.rsqrt(jnp.mean(xf * xf, axis=1, keepdims=True) + EPSILON)
    total = jnp.sum(gn * xf * inv, axis=0, keepdims=True)
    for i in range(8):
        h0[i : i + 1, :] = total[:, 128 * i : 128 * (i + 1)]
    for slot, d in enumerate(SIBLINGS):
        push(GAIN, h0, h1.at[slot], x_peer[d])
    sum_half(4)
    sum_one(3)
    s = gn * gain_ref[...]
    back = inv * (s - xf * inv * inv * jnp.mean(s * xf, axis=1, keepdims=True))
    gin_v[...] = (grad_ref[...].astype(F32) + tile_of(back)).astype(BF16)
    store_gin = pltpu.make_async_copy(gin_v, gin_hbm, local_sem.at[1])
    store_gin.start()

    sum_half(5)
    sum_one(4)
    sum_two(0)
    arrive(GAIN, h1)
    t1[...] = h0[...] + h1[0] + h1[1] + h1[2]
    for slot, d in enumerate(SIBLINGS):
        push(GAIN + 1, t1, h2.at[slot], y_peer[d])
    sum_one(5)
    arrive(GAIN + 1, h2)
    t2[...] = t1[...] + h2[0] + h2[1] + h2[2]
    for slot, d in enumerate(FAR_FIRST):
        push(GAIN + 2, t2, h3.at[slot], z_peer[d])
    sum_two(1)

    arrive(GAIN + 2, h3)
    tot = t2[...]
    for slot in range(7):
        tot = tot + h3[slot]
    t3[...] = tot
    push(GAIN + 3, t3, h4, partner)
    for batch in range(2):
        arrive(THREE + batch, r3.at[batch])
        acc = s2[batch, z].astype(F32)
        for slot in range(7):
            acc = acc + r3[batch, slot].astype(F32)
        acc = acc * (ALL_TOKENS ** (-0.5))
        fin[0, batch] = acc[0:4]
        fin[1, batch] = acc[4:8]
    push(FOUR, fin.at[1 - core], r4, partner)

    for c, (b, rows) in enumerate(pieces):
        leave(N_NEAR + c, n_ext.at[0, b, rows, :])
    for b in range(2):
        leave(N_FAR + b, n_ext.at[0, b])
        leave(G_NEAR + b, g_ext.at[0, b])
        leave(G_FAR + b, g_ext.at[0, b])
    for sem, ext in ((N_MID, n_ext), (G_MID, g_ext)):
        leave(sem, ext.at[0, 2:4])
        leave(sem + 1, ext.at[1:3, 2:4])
    leave(A2, a2.at[0])
    for g in range(GROUPS + 1):
        leave(STAT + g, st_ext.at[g])
    for u in range(UNITS):
        leave(PAIR + u, b_other.at[u])
        leave(ONE + u, r1.at[u])
        leave(HALF + u, r_half.at[u])
        leave(TWO + u, r2.at[u])
    for batch in range(2):
        leave(THREE + batch, r3.at[batch])
    for i, ref in enumerate((h1, h2, h3, h4)):
        leave(GAIN + i, ref)
    store_out.wait()
    store_gin.wait()

    arrive(GAIN + 3, h4)
    summed = (t3[...] + h4[...]) * (ALL_TOKENS ** (-0.5))
    t1[...] = summed
    gg_ref[...] = pltpu.roll(t1[pl.ds(gx, 1), :], lax.rem(128 - 4 * gy, 128), 1)
    arrive(FOUR, r4)
    leave(FOUR, r4)
    for batch in range(2):
        mine, other = fin[core, batch], r4[batch]
        is_first = jnp.broadcast_to(core, mine.shape) == 0
        halves = (jnp.where(is_first, mine, other), jnp.where(is_first, other, mine))
        for j in range(3):
            u = 3 * batch + j
            for i in range(2):
                base = GW * (2 * u + i) if u < 2 else D * (1 + i) + GW * (u - 2)
                come = UW * j + HW * i
                for half in range(2):
                    to = base + HW * half
                    wg_ref[:, to : to + HW] = halves[half][:, come : come + HW]


def layer_call(mask, fields, grad_out, gain, w):
    dma = pltpu.SemaphoreType.DMA
    vm = pltpu.VMEM
    tile = (8, 128)
    stack = (GROUP * OWN, EXT)
    return pl.pallas_call(
        layer_kernel,
        out_shape=(
            jax.ShapeDtypeStruct(fields.shape, BF16),
            jax.ShapeDtypeStruct(fields.shape, BF16),
            jax.ShapeDtypeStruct((4, 3 * D), F32),
            jax.ShapeDtypeStruct((1, 128), F32),
        ),
        in_specs=[SM, VM, VM, VM, ANY],
        out_specs=(ANY, ANY, VM, VM),
        scratch_shapes=[
            vm((D, 3 * D), BF16),
            vm((3, 4, INSIDE, D), BF16), vm((3, 4, INSIDE, D), BF16),
            vm((2, D, OWN), BF16),
            vm((EXT, D), BF16), vm((EXT, D), BF16), vm((EXT, D), BF16),
            vm((OWN, D), BF16), vm((OWN, D), BF16), vm((OWN, D), BF16),
            vm(stack, F32), vm(stack, F32), vm(stack, BF16), vm(stack, BF16),
            vm((GROUPS + 1,) + tile, F32), vm((GROUPS + 1, 8) + tile, F32),
            vm(fields.shape, BF16), vm(fields.shape, BF16),
            vm((UNITS, 2, OWN, UW), BF16), vm((UNITS, OWN, UW), BF16),
            vm((UNITS, 4, 4, 2, 32, UW), BF16),
            vm((UNITS, 2, 2, 4, 32, UW), BF16),
            vm((UNITS, 2, 4, 32, UW), BF16),
            vm((UNITS, 2, 4, 32, UW), BF16),
            vm((UNITS, 2, 4, 32, UW), BF16),
            vm((UNITS, 2, 3, 32, UW), BF16),
            vm((2, 8, 8, 3 * UW), BF16),
            vm((2, 7, 8, 3 * UW), BF16),
            vm((2, 2, 4, 3 * UW), F32),
            vm((2, 4, 3 * UW), F32),
            vm(tile, F32), vm((3,) + tile, F32),
            vm(tile, F32), vm((3,) + tile, F32),
            vm(tile, F32), vm((7,) + tile, F32),
            vm(tile, F32), vm(tile, F32),
            dma((3,)), dma((SEMS,)), dma((SEMS,)),
        ],
        compiler_params=pltpu.CompilerParams(
            collective_id=0, has_side_effects=True, vmem_limit_bytes=VMEM_LIMIT
        ),
        name="layer",
    )(mask, fields, grad_out, gain, w)


def finish_kernel(out_in, gin_in, wg_in, gg_in, out, gin, wg, gg):
    out[...] = out_in[...]
    gin[...] = gin_in[...]
    wg[...] = wg_in[...]
    for i in range(4):
        gg[i] = gg_in[0, i]


def finish_call(output, grad_in, w_grad, gains):
    return pl.pallas_call(
        finish_kernel,
        out_shape=(
            jax.ShapeDtypeStruct(output.shape, BF16),
            jax.ShapeDtypeStruct(grad_in.shape, BF16),
            jax.ShapeDtypeStruct(w_grad.shape, F32),
            jax.ShapeDtypeStruct((4,), F32),
        ),
        in_specs=[VM] * 4,
        out_specs=(VM, VM, VM, SM),
        name="finish",
    )(output, grad_in, w_grad, gains)


def per_device(fields, grad_out, norm_gain, w_qkv, brick_mask):
    made = layer_call(
        brick_mask.reshape(2, 8), fields, grad_out, norm_gain.reshape(1, D), w_qkv
    )
    return finish_call(*made)


def solution(mesh):
    placed = (P("gx", "gy", None), P("gx", "gy", None), P(), P(), P("gx", "gy", None))
    return jax.shard_map(
        per_device,
        mesh=mesh,
        in_specs=placed,
        out_specs=(
            P("gx", "gy", None),
            P("gx", "gy", None),
            P(("gx", "gy"), None),
            P(("gx", "gy")),
        ),
        check_vma=False,
    )
```
